128 devices in a mesh: group: 32 (over y, x, core), pos: 4 (over z).
Axes of the slice: x: 4, y: 4, z: 4, core: 2. Of those that a mesh axis runs over, the one named last changes fastest.
Arguments:
- features: bfloat16 [1536, 256, 256], P(('group', 'pos')), may hold values from -6 to 6
- gain_attn: float32 [256], replicated, may hold values from 0.1 to 1.9
- w_query: bfloat16 [256, 256], replicated, as said below
- w_key: bfloat16 [256, 256], replicated, as said below
- w_value: bfloat16 [256, 256], replicated, may hold values from -0.375 to 0.375
- w_out: bfloat16 [256, 256], replicated, may hold values from -0.375 to 0.375
- gain_ffn: float32 [256], replicated, may hold values from 0.1 to 1.9
- w_up: bfloat16 [256, 1024], replicated, may hold values from -0.375 to 0.375
- w_down: bfloat16 [1024, 256], replicated, may hold values from -0.1875 to 0.1875
- counts: int32 [6], replicated, may hold values from 16 to 256, as said below
- offsets: int32 [6], replicated, may hold values from 0 to 1520, as said below
Outputs:
- result: bfloat16 [1536, 256, 256], P(('group', 'pos'))
The draws below stay inside these ranges and needn't reach their ends.
Inputs may be any that keep to these rules, and one draw needn't show every extreme that they name: `counts`: each mixture has 16 to 256 groups, and one mixture has exactly 256. Mixture m occupies slots offsets[m] to offsets[m] + counts[m] - 1; the mixtures follow one another in order without intersection. `w_query`: a dense matrix of independent entries. `w_key`: a dense matrix of independent entries.
All inputs are finite; a program needn't handle non-finite values.
Results may differ from the reference program's by a relative error of at most 0.0065.
Values may be sent and summed in bfloat16 or wider, within the bound.
A program may use at most 192 MiB of HBM per device.

```python
import math
import jax
import jax.numpy as jnp
from jax import lax

D = 256
HEADS = 8
FF = 1024
K = 256
MIX = 6
NCH = 1536
MAXC = 256
MINC = 16


def group_layout(key):
    base = jax.random.fold_in(key, 31)
    first, second, third = jax.random.split(base, 3)
    counts = jax.random.randint(first, (MIX,), MINC, MAXC + 1, dtype=jnp.int32)
    chosen = jax.random.randint(second, (), 0, MIX, dtype=jnp.int32)
    counts = jnp.where(jnp.arange(MIX, dtype=jnp.int32) == chosen, MAXC, counts).astype(jnp.int32)
    spare = NCH - jnp.sum(counts)
    shares = jax.random.randint(third, (MIX + 1,), 1, 100, dtype=jnp.int32)
    gaps = spare * shares // jnp.sum(shares)
    offsets = jnp.cumsum(gaps[:MIX]) + jnp.cumsum(counts) - counts
    return (counts.astype(jnp.int32), offsets.astype(jnp.int32))


def draw_counts(key, part):
    return group_layout(key)[0]


def draw_offsets(key, part):
    return group_layout(key)[1]


def paired_normals(key):
    shared = jax.random.normal(jax.random.fold_in(key, 41), (D, D), jnp.float32)
    other = jax.random.normal(jax.random.fold_in(key, 43), (D, D), jnp.float32)
    return (shared, other)


def draw_w_query(key, part):
    shared, other = paired_normals(key)
    return (shared / D ** 0.5).astype(jnp.bfloat16)


def draw_w_key(key, part):
    shared, other = paired_normals(key)
    return (other / D ** 0.5).astype(jnp.bfloat16)


def shard_levels(rng, dims, cuts, smallest, high):
    level, own = 1.0, jax.random.fold_in(rng, 6)
    for dim, parts in cuts:
        draws = jnp.exp(jax.random.uniform(jax.random.fold_in(own, dim), (parts,), jnp.float32, smallest / len(cuts), high / len(cuts)))
        level = level * jnp.repeat(draws, dims[dim] // parts).reshape([-1 if axis == dim else 1 for axis in range(len(dims))])
    return level


def gaussian(stream_key, shape, scale, most, shards=(), kind=jnp.bfloat16):
    array = jax.random.normal(stream_key, shape, jnp.float32) * scale
    if len(shards) > 0:
        array = shard_levels(stream_key, shape, shards, -0.22, 0.18) * array
    return jnp.clip(array, min=-most, max=most).astype(kind)


def setup_inputs(seed: int = 0) -> dict:
    seeds = jax.random.split(jax.random.key(seed), 12)
    return {
        "features": gaussian(seeds[0], (NCH, K, D), 1.0, 6.0, ((0, 128),)),
        "gain_attn": jnp.clip(1.0 + 0.18 * jax.random.normal(seeds[1], (D,), jnp.float32), 0.1, 1.9),
        "w_query": draw_w_query(jax.random.fold_in(seeds[11], 71), 0),
        "w_key": draw_w_key(jax.random.fold_in(seeds[11], 71), 0),
        "w_value": gaussian(seeds[4], (D, D), D ** -0.5, 0.375),
        "w_out": gaussian(seeds[5], (D, D), D ** -0.5, 0.375),
        "gain_ffn": jnp.clip(1.0 + 0.18 * jax.random.normal(seeds[6], (D,), jnp.float32), 0.1, 1.9),
        "w_up": gaussian(seeds[7], (D, FF), D ** -0.5, 0.375),
        "w_down": gaussian(seeds[8], (FF, D), FF ** -0.5, 0.1875),
        "counts": draw_counts(jax.random.fold_in(seeds[11], 71), 0),
        "offsets": draw_offsets(jax.random.fold_in(seeds[11], 71), 0),
    }


epsilon = 1e-05
masked_value = -1e+30

def segment_ids(counts, offsets, slots_total):
    slots = jnp.arange(slots_total, dtype=jnp.int32)[:, None]
    inside = (slots >= offsets[None, :]) & (slots < offsets[None, :] + counts[None, :])
    labels = jnp.arange(counts.shape[0], dtype=jnp.int32)[None, :] + 1
    return lax.optimization_barrier(jnp.sum(jnp.where(inside, labels, 0), axis=1)).astype(jnp.int32) - 1

def layer_norm(values, gain):
    floats = values.astype(jnp.float32)
    average = lax.optimization_barrier(jnp.mean(floats, axis=-1, keepdims=True))
    centred = floats - average
    spread = lax.optimization_barrier(jnp.mean(centred * centred, axis=-1, keepdims=True))
    return (centred * lax.rsqrt(spread + epsilon) * gain.astype(jnp.float32)).astype(jnp.bfloat16)

def feed_forward(middle, gain_ffn, w_up, w_down):
    second = layer_norm(middle, gain_ffn)
    hidden = jnp.maximum(jnp.dot(second, w_up, preferred_element_type=jnp.float32), 0.0).astype(jnp.bfloat16)
    return (middle.astype(jnp.float32) + jnp.dot(hidden, w_down, preferred_element_type=jnp.float32)).astype(jnp.bfloat16)

def reference(features, gain_attn, w_query, w_key, w_value, w_out, gain_ffn, w_up, w_down, counts, offsets):
    labels = segment_ids(counts, offsets, NCH)
    living = labels >= 0
    allowed = (labels[:, None] == labels[None, :]) & living[:, None]
    head_dim = D // HEADS
    scale = 1.0 / math.sqrt(head_dim)

    def one_position(column):
        normed = layer_norm(column, gain_attn)
        query = jnp.dot(normed, w_query, preferred_element_type=jnp.float32).astype(jnp.bfloat16).reshape(NCH, HEADS, head_dim)
        keys = jnp.dot(normed, w_key, preferred_element_type=jnp.float32).astype(jnp.bfloat16).reshape(NCH, HEADS, head_dim)
        values = jnp.dot(normed, w_value, preferred_element_type=jnp.float32).astype(jnp.bfloat16).reshape(NCH, HEADS, head_dim)
        scores = jnp.einsum('qhe,khe->hqk', query.astype(jnp.float32), keys.astype(jnp.float32)) * scale
        scores = jnp.where(allowed[None], scores, masked_value)
        highest = lax.optimization_barrier(jnp.max(scores, axis=-1, keepdims=True))
        exponent = jnp.exp(scores - highest)
        total = lax.optimization_barrier(jnp.sum(exponent, axis=-1, keepdims=True))
        weights = (exponent / total).astype(jnp.bfloat16)
        context = jnp.einsum('hqk,khe->qhe', weights.astype(jnp.float32), values.astype(jnp.float32)).astype(jnp.bfloat16).reshape(NCH, D)
        context = jnp.where(living[:, None], context, jnp.zeros_like(context))
        middle = (column.astype(jnp.float32) + jnp.dot(context, w_out, preferred_element_type=jnp.float32)).astype(jnp.bfloat16)
        return feed_forward(middle, gain_ffn, w_up, w_down)
    outputs = lax.map(one_position, jnp.swapaxes(features, 0, 1))
    return jnp.swapaxes(outputs, 0, 1)
```

```python
import functools
import math

import jax
import jax.numpy as jnp
import numpy as np
from jax import lax
from jax.experimental import pallas as pl
from jax.experimental.pallas import tpu as pltpu
from jax.sharding import PartitionSpec as P

HEADS = 8
MIX = 6
MAXC = 256
LANES = 128
PAIR = 2

epsilon = 1e-05
BF = jnp.bfloat16
F32 = jnp.float32
MESH = pl.DeviceIdType.MESH


def one_hot_rows(picks, width):
    matrix = np.zeros((len(picks), width), np.float32)
    matrix[np.arange(len(picks)), picks] = 1.0
    return matrix


def permutations(groups, eight):
    pack = [
        half * groups * 2 * eight + slot * 2 * eight + PAIR * device + pos
        for pos in range(PAIR)
        for device in range(eight)
        for half in range(2)
        for slot in range(groups)
    ]
    unpack = [
        device * 2 * groups + half * groups + slot
        for half in range(2)
        for device in range(eight)
        for slot in range(groups)
    ]
    final = [
        pos * eight * groups + device * groups + slot
        for slot in range(groups)
        for device in range(eight)
        for pos in range(PAIR)
    ]
    unpack_matrix = one_hot_rows(unpack, 2 * eight * groups)
    return (
        one_hot_rows(pack, 2 * 2 * eight * groups),
        unpack_matrix,
        unpack_matrix.T.copy(),
        one_hot_rows(final, PAIR * eight * groups),
    )


def dot(left, right):
    return jnp.dot(left, right, preferred_element_type=F32)


def dot_nt(left, right):
    return lax.dot_general(
        left, right, (((1,), (1,)), ((), ())), preferred_element_type=F32
    )


def layer_norm(floats, gain):
    average = jnp.mean(floats, axis=-1, keepdims=True)
    centred = floats - average
    spread = jnp.mean(centred * centred, axis=-1, keepdims=True)
    return (centred * lax.rsqrt(spread + epsilon) * gain).astype(BF)


def halves(left, right):
    low = jnp.concatenate([left[:, :LANES], right[:, :LANES]], axis=1)
    high = jnp.concatenate([left[:, LANES:], right[:, LANES:]], axis=1)
    return jnp.concatenate([low, high], axis=0)


def unhalves(rows):
    count = rows.shape[0] // 2
    left = jnp.concatenate([rows[:count, :LANES], rows[count:, :LANES]], axis=1)
    right = jnp.concatenate([rows[:count, LANES:], rows[count:, LANES:]], axis=1)
    return jnp.concatenate([left, right], axis=0)


def kernel(
    sizes,
    counts,
    offsets,
    features,
    gain_attn,
    w_query,
    w_key,
    w_value,
    w_out,
    gain_ffn,
    w_up,
    w_down,
    pack_m,
    unpack_m,
    repack_m,
    final_m,
    result,
    send_in,
    recv_in,
    send_out,
    recv_out,
    slots_x,
    slots_n,
    gather_m,
    scatter_m,
    context_t,
    wq_t,
    wv_t,
    early,
    in_sems,
    out_sems,
):
    devices, axis_sizes = sizes
    groups = features.shape[0]
    width = features.shape[2]
    slots = devices * groups
    eight = 8
    block = eight * groups
    steps = devices // (2 * eight)
    group_at = lax.axis_index("group")
    pos_at = lax.axis_index("pos")
    me = group_at * axis_sizes[1] + pos_at

    barrier = pltpu.get_barrier_semaphore()

    def greet(step, carry):
        other = lax.rem(me + step, devices)
        pl.semaphore_signal(
            barrier,
            inc=1,
            device_id=(other // axis_sizes[1], lax.rem(other, axis_sizes[1])),
            device_id_type=MESH,
        )
        return carry

    lax.fori_loop(1, devices, greet, 0)

    def pack(step, carry):
        start = pl.multiple_of(step * 4 * eight, 4 * eight)
        left = features[:, pl.ds(start, 2 * eight), :].reshape(2 * block, width)
        right = features[:, pl.ds(pl.multiple_of(start + 2 * eight, 2 * eight), 2 * eight), :]
        right = right.reshape(2 * block, width)
        rows = dot(pack_m[...], halves(left, right)).astype(BF)
        for pos in range(PAIR):
            part = rows[pos * 2 * block : (pos + 1) * 2 * block]
            for side in range(2):
                send_in[pos, pl.ds(step * 2 * eight + side * eight, eight)] = part[
                    :, side * LANES : (side + 1) * LANES
                ].reshape(eight, 2 * groups, LANES)
        return carry

    lax.fori_loop(0, steps, pack, 0)
    pl.semaphore_wait(barrier, devices - 1)

    def exchange(pos, source, target, sems):
        own = pltpu.make_async_copy(
            source.at[pos, me], target.at[pos, me], sems.at[2 * PAIR + pos]
        )
        own.start()

        def send(step, carry):
            other = lax.rem(me + step * 37, devices)
            pltpu.make_async_remote_copy(
                src_ref=source.at[pos, other],
                dst_ref=target.at[pos, me],
                send_sem=sems.at[pos],
                recv_sem=sems.at[PAIR + pos],
                device_id=(other // axis_sizes[1], lax.rem(other, axis_sizes[1])),
                device_id_type=MESH,
            ).start()
            return carry

        lax.fori_loop(1, devices, send, 0)

    def arrived(pos, target, sems):
        others = target.at[pos, pl.ds(0, devices - 1)]
        pltpu.make_async_copy(others, others, sems.at[PAIR + pos]).wait()
        pltpu.make_async_copy(
            target.at[pos, me], target.at[pos, me], sems.at[2 * PAIR + pos]
        ).wait()

    def sent(pos, source, sems):
        others = source.at[pos, pl.ds(0, devices - 1)]
        pltpu.make_async_copy(others, others, sems.at[pos]).wait()

    for pos in range(PAIR):
        exchange(pos, send_in, recv_in, in_sems)

    def select_in(mixture, carry):
        row = lax.broadcasted_iota(jnp.int32, (MAXC, 1), 0)
        pick = jnp.where(row < counts[mixture], row, 0) + offsets[mixture]
        column = lax.broadcasted_iota(jnp.int32, (MAXC, slots), 1)
        gather_m[mixture] = jnp.where(column == pick, 1.0, 0.0).astype(BF)
        return carry

    lax.fori_loop(0, MIX, select_in, 0)

    def select_out(step, carry):
        start = pl.multiple_of(step * 2 * block, 2 * block)
        slot = start + lax.broadcasted_iota(jnp.int32, (2 * block, 1), 0)
        pick = jnp.full((2 * block, 1), -1, jnp.int32)
        for mixture in range(MIX):
            place = slot - offsets[mixture]
            inside = (place >= 0) & (place < counts[mixture])
            pick = jnp.where(inside, place + mixture * MAXC, pick)
        column = lax.broadcasted_iota(jnp.int32, (2 * block, MIX * MAXC), 1)
        scatter_m[pl.ds(start, 2 * block), :] = jnp.where(column == pick, 1.0, 0.0).astype(BF)
        return carry

    lax.fori_loop(0, steps, select_out, 0)
    wq_t[...] = w_query[...].astype(F32).T.astype(BF)
    wv_t[...] = w_value[...].astype(F32).T.astype(BF)

    head = width // HEADS
    scale = math.log2(math.e) / math.sqrt(head)

    def pair_of_blocks(buffer, pos, step):
        sides = [
            buffer[pos, pl.ds(step * 2 * eight + side * eight, eight)].reshape(2 * block, LANES)
            for side in range(2)
        ]
        return unhalves(dot(unpack_m[...], jnp.concatenate(sides, axis=1)))

    for pos in range(PAIR):
        arrived(pos, recv_in, in_sems)

        def unpack(step, carry):
            start = pl.multiple_of(step * 2 * block, 2 * block)
            rows = pair_of_blocks(recv_in, pos, step)
            slots_x[pl.ds(start, 2 * block), :] = rows.astype(BF)
            slots_n[pl.ds(start, 2 * block), :] = layer_norm(rows, gain_attn[...])
            return carry

        lax.fori_loop(0, steps, unpack, 0)

        def attend(mixture, carry):
            normed = dot(gather_m[mixture], slots_n[...]).astype(BF)
            query_t = dot_nt(wq_t[...], normed).astype(BF)
            keys = dot(normed, w_key[...]).astype(BF)
            values_t = dot_nt(wv_t[...], normed)
            valid = lax.broadcasted_iota(jnp.int32, (1, MAXC), 1) < counts[mixture]
            values_t = jnp.where(valid, values_t, 0.0).astype(BF)
            ones = jnp.broadcast_to(jnp.where(valid, 1.0, 0.0), (16, MAXC)).astype(BF)
            lane_head = lax.broadcasted_iota(jnp.int32, (1, width), 1) // head
            at = pl.multiple_of(mixture * MAXC, MAXC)
            for h in range(HEADS):
                mask = jnp.where(lane_head == h, 1.0, 0.0).astype(BF)
                scores = dot(keys * mask, query_t)
                highest = jnp.max(scores, axis=0, keepdims=True)
                exponent = jnp.exp2((scores - highest) * scale).astype(BF)
                part = jnp.concatenate([values_t[h * head : (h + 1) * head], ones], axis=0)
                sums = dot(part, exponent)
                context_t[h * head : (h + 1) * head, pl.ds(at, MAXC)] = (
                    sums[:head] / sums[head : head + 1]
                ).astype(BF)
            return carry

        lax.fori_loop(0, MIX, attend, 0)

        def combine(step, carry):
            start = pl.multiple_of(step * 2 * block, 2 * block)
            context = dot_nt(scatter_m[pl.ds(start, 2 * block), :], context_t[...]).astype(BF)
            middle = slots_x[pl.ds(start, 2 * block), :].astype(F32) + dot(context, w_out[...])
            middle = middle.astype(BF)
            rows = dot(repack_m[...], halves(middle[:block], middle[block:])).astype(BF)
            for side in range(2):
                send_out[pos, pl.ds(step * 2 * eight + side * eight, eight)] = rows[
                    :, side * LANES : (side + 1) * LANES
                ].reshape(eight, 2 * groups, LANES)
            return carry

        lax.fori_loop(0, steps, combine, 0)
        exchange(pos, send_out, recv_out, out_sems)

    for pos in range(PAIR):
        arrived(pos, recv_out, out_sems)

        def finish(step, carry):
            start = pl.multiple_of(step * 2 * block, 2 * block)
            rows = pair_of_blocks(recv_out, pos, step)
            second = layer_norm(rows, gain_ffn[...])
            hidden = jnp.maximum(dot(second, w_up[...]), 0.0).astype(BF)
            rows = (rows + dot(hidden, w_down[...])).astype(BF)
            if pos == 0:
                early[pl.ds(start, 2 * block), :] = rows
            else:
                before = early[pl.ds(start, 2 * block), :]
                for side in range(2):
                    cut = slice(side * block, (side + 1) * block)
                    both = jnp.concatenate([before[cut], rows[cut]], axis=0)
                    both = dot(final_m[...], both).astype(BF)
                    place = pl.multiple_of(step * 4 * eight + side * 2 * eight, 2 * eight)
                    result[:, pl.ds(place, 2 * eight), :] = both.reshape(
                        groups, 2 * eight, width
                    )
            return carry

        lax.fori_loop(0, steps, finish, 0)

    for pos in range(PAIR):
        sent(pos, send_in, in_sems)
        sent(pos, send_out, out_sems)


def local(
    axis_sizes,
    features,
    gain_attn,
    w_query,
    w_key,
    w_value,
    w_out,
    gain_ffn,
    w_up,
    w_down,
    counts,
    offsets,
):
    groups, positions, width = features.shape
    devices = axis_sizes[0] * axis_sizes[1]
    slots = groups * devices
    matrices = [jnp.asarray(m, BF) for m in permutations(groups, 8)]
    vmem = pl.BlockSpec(memory_space=pltpu.VMEM)
    smem = pl.BlockSpec(memory_space=pltpu.SMEM)
    link = pltpu.VMEM((PAIR, devices, 2 * groups, LANES), BF)
    return pl.pallas_call(
        functools.partial(kernel, (devices, axis_sizes)),
        out_shape=jax.ShapeDtypeStruct(features.shape, BF),
        in_specs=[smem, smem] + [vmem] * 13,
        out_specs=vmem,
        scratch_shapes=[
            link,
            link,
            link,
            link,
            pltpu.VMEM((slots, width), BF),
            pltpu.VMEM((slots, width), BF),
            pltpu.VMEM((MIX, MAXC, slots), BF),
            pltpu.VMEM((slots, MIX * MAXC), BF),
            pltpu.VMEM((width, MIX * MAXC), BF),
            pltpu.VMEM((width, width), BF),
            pltpu.VMEM((width, width), BF),
            pltpu.VMEM((slots, width), BF),
            pltpu.SemaphoreType.DMA((3 * PAIR,)),
            pltpu.SemaphoreType.DMA((3 * PAIR,)),
        ],
        compiler_params=pltpu.CompilerParams(
            collective_id=0, has_side_effects=True, vmem_limit_bytes=56 << 20
        ),
    )(
        counts,
        offsets,
        features,
        gain_attn.reshape(1, width),
        w_query,
        w_key,
        w_value,
        w_out,
        gain_ffn.reshape(1, width),
        w_up,
        w_down,
        *matrices,
    )


def solution(mesh):
    axis_sizes = (mesh.shape["group"], mesh.shape["pos"])
    return jax.shard_map(
        functools.partial(local, axis_sizes),
        mesh=mesh,
        in_specs=(P(("group", "pos"), None, None),) + (P(),) * 10,
        out_specs=P(("group", "pos"), None, None),
        check_vma=False,
    )
```

```python
import functools
import math

import jax
import jax.numpy as jnp
import numpy as np
from jax import lax
from jax.experimental import pallas as pl
from jax.experimental.pallas import tpu as pltpu
from jax.sharding import PartitionSpec as P

HEADS = 8
MIX = 6
MAXC = 256
LANES = 128
PAIR = 2

epsilon = 1e-05
BF = jnp.bfloat16
F32 = jnp.float32
MESH = pl.DeviceIdType.MESH


def one_hot_rows(picks, width):
    matrix = np.zeros((len(picks), width), np.float32)
    matrix[np.arange(len(picks)), picks] = 1.0
    return matrix


def permutations(groups, eight):
    pack = [
        half * groups * 2 * eight + slot * 2 * eight + PAIR * device + pos
        for pos in range(PAIR)
        for device in range(eight)
        for half in range(2)
        for slot in range(groups)
    ]
    unpack = [
        device * 2 * groups + half * groups + slot
        for half in range(2)
        for device in range(eight)
        for slot in range(groups)
    ]
    final = [
        pos * eight * groups + device * groups + slot
        for slot in range(groups)
        for device in range(eight)
        for pos in range(PAIR)
    ]
    unpack_matrix = one_hot_rows(unpack, 2 * eight * groups)
    return (
        one_hot_rows(pack, 2 * 2 * eight * groups),
        unpack_matrix,
        unpack_matrix.T.copy(),
        one_hot_rows(final, PAIR * eight * groups),
    )


def dot(left, right):
    return jnp.dot(left, right, preferred_element_type=F32)


def dot_nt(left, right):
    return lax.dot_general(
        left, right, (((1,), (1,)), ((), ())), preferred_element_type=F32
    )


def layer_norm(floats, gain):
    average = jnp.mean(floats, axis=-1, keepdims=True)
    centred = floats - average
    spread = jnp.mean(centred * centred, axis=-1, keepdims=True)
    return (centred * lax.rsqrt(spread + epsilon) * gain).astype(BF)


def halves(left, right):
    low = jnp.concatenate([left[:, :LANES], right[:, :LANES]], axis=1)
    high = jnp.concatenate([left[:, LANES:], right[:, LANES:]], axis=1)
    return jnp.concatenate([low, high], axis=0)


def unhalves(rows):
    count = rows.shape[0] // 2
    left = jnp.concatenate([rows[:count, :LANES], rows[count:, :LANES]], axis=1)
    right = jnp.concatenate([rows[:count, LANES:], rows[count:, LANES:]], axis=1)
    return jnp.concatenate([left, right], axis=0)


def kernel(
    sizes,
    counts,
    offsets,
    features,
    gain_attn,
    w_query,
    w_key,
    w_value,
    w_out,
    gain_ffn,
    w_up,
    w_down,
    pack_m,
    unpack_m,
    repack_m,
    final_m,
    result,
    send_in,
    recv_in,
    send_out,
    recv_out,
    slots_x,
    slots_n,
    gather_m,
    scatter_m,
    context_t,
    wqv_t,
    is_valid,
    query_t,
    keys,
    values_t,
    scores_even,
    scores_odd,
    highest_even,
    highest_odd,
    early,
    in_sems,
    out_sems,
):
    devices, axis_sizes = sizes
    groups = features.shape[0]
    width = features.shape[2]
    slots = devices * groups
    eight = 8
    block = eight * groups
    wide = 4
    steps = devices // (wide * eight)
    group_at = lax.axis_index("group")
    pos_at = lax.axis_index("pos")
    me = group_at * axis_sizes[1] + pos_at

    barrier = pltpu.get_barrier_semaphore()

    def greet(step, carry):
        other = lax.rem(me + step, devices)
        pl.semaphore_signal(
            barrier,
            inc=1,
            device_id=(other // axis_sizes[1], lax.rem(other, axis_sizes[1])),
            device_id_type=MESH,
        )
        return carry

    lax.fori_loop(1, devices, greet, 0)

    def pack(step, carry):
        start = pl.multiple_of(step * 4 * eight, 4 * eight)
        left = features[:, pl.ds(start, 2 * eight), :].reshape(2 * block, width)
        right = features[:, pl.ds(pl.multiple_of(start + 2 * eight, 2 * eight), 2 * eight), :]
        right = right.reshape(2 * block, width)
        rows = dot(pack_m[...], halves(left, right)).astype(BF)
        for pos in range(PAIR):
            part = rows[pos * 2 * block : (pos + 1) * 2 * block]
            for side in range(2):
                send_in[pos, pl.ds(step * 2 * eight + side * eight, eight)] = part[
                    :, side * LANES : (side + 1) * LANES
                ].reshape(eight, 2 * groups, LANES)
        return carry

    lax.fori_loop(0, devices // (2 * eight), pack, 0)
    pl.semaphore_wait(barrier, devices - 1)

    def exchange(pos, source, target, sems):
        own = pltpu.make_async_copy(
            source.at[pos, me], target.at[pos, me], sems.at[2 * PAIR + pos]
        )
        own.start()
        along = [lax.rem(pos_at + hop, axis_sizes[1]) for hop in range(axis_sizes[1])]

        def send(group, place):
            pltpu.make_async_remote_copy(
                src_ref=source.at[pos, group * axis_sizes[1] + place],
                dst_ref=target.at[pos, me],
                send_sem=sems.at[pos],
                recv_sem=sems.at[PAIR + pos],
                device_id=(group, place),
                device_id_type=MESH,
            ).start()

        for place in along[1:]:
            send(group_at, place)

        def send_group(step, carry):
            group = lax.rem(group_at + step * 13, axis_sizes[0])
            for place in along:
                send(group, place)
            return carry

        lax.fori_loop(1, axis_sizes[0], send_group, 0)

    def arrived(pos, target, sems):
        others = target.at[pos, pl.ds(0, devices - 1)]
        pltpu.make_async_copy(others, others, sems.at[PAIR + pos]).wait()
        pltpu.make_async_copy(
            target.at[pos, me], target.at[pos, me], sems.at[2 * PAIR + pos]
        ).wait()

    def sent(pos, source, sems):
        others = source.at[pos, pl.ds(0, devices - 1)]
        pltpu.make_async_copy(others, others, sems.at[pos]).wait()

    for pos in range(PAIR):
        exchange(pos, send_in, recv_in, in_sems)

    def select_in(mixture, carry):
        row = lax.broadcasted_iota(jnp.int32, (MAXC, 1), 0)
        pick = jnp.where(row < counts[mixture], row, 0) + offsets[mixture]
        column = lax.broadcasted_iota(jnp.int32, (MAXC, slots), 1)
        gather_m[pl.ds(pl.multiple_of(mixture * MAXC, MAXC), MAXC), :] = jnp.where(column == pick, 1.0, 0.0).astype(BF)
        return carry

    lax.fori_loop(0, MIX, select_in, 0)

    def select_out(step, carry):
        start = pl.multiple_of(step * 2 * block, 2 * block)
        slot = start + lax.broadcasted_iota(jnp.int32, (2 * block, 1), 0)
        pick = jnp.full((2 * block, 1), -1, jnp.int32)
        for mixture in range(MIX):
            place = slot - offsets[mixture]
            inside = (place >= 0) & (place < counts[mixture])
            pick = jnp.where(inside, place + mixture * MAXC, pick)
        column = lax.broadcasted_iota(jnp.int32, (2 * block, MIX * MAXC), 1)
        scatter_m[pl.ds(start, 2 * block), :] = jnp.where(column == pick, 1.0, 0.0).astype(BF)
        return carry

    lax.fori_loop(0, devices // (2 * eight), select_out, 0)
    head = width // HEADS
    scale = math.log2(math.e) / math.sqrt(head)
    wqv_t[0:width, :] = w_query[...].astype(F32).T.astype(BF)
    wqv_t[width:, :] = w_value[...].astype(F32).T.astype(BF)
    column = lax.broadcasted_iota(jnp.int32, (1, MIX * MAXC), 1)
    valid = jnp.zeros((1, MIX * MAXC), F32)
    for mixture in range(MIX):
        inside = (column >= mixture * MAXC) & (column < mixture * MAXC + counts[mixture])
        valid = jnp.where(inside, 1.0, valid)
    is_valid[...] = valid
    for h in range(HEADS):
        values_t[h, head:, :] = jnp.broadcast_to(valid, (16, MIX * MAXC)).astype(BF)

    def blocks_of(buffer, pos, step):
        rows = []
        for two in range(wide // 2):
            first = (step * (wide // 2) + two) * 2 * eight
            sides = [
                buffer[pos, pl.ds(first + side * eight, eight)].reshape(2 * block, LANES)
                for side in range(2)
            ]
            rows.append(unhalves(dot(unpack_m[...], jnp.concatenate(sides, axis=1))))
        return jnp.concatenate(rows, axis=0)

    scores = (scores_even, scores_odd)
    highest = (highest_even, highest_odd)

    def scores_of(mixture, h, slot):
        at = pl.multiple_of(mixture * MAXC, MAXC)
        lane_head = lax.broadcasted_iota(jnp.int32, (1, width), 1) // head
        mask = jnp.where(lane_head == h, 1.0, 0.0).astype(BF)
        logits = dot(keys[pl.ds(at, MAXC), :] * mask, query_t[:, pl.ds(at, MAXC)])
        scores[slot][h] = logits
        highest[slot][h : h + 1, :] = jnp.max(logits, axis=0, keepdims=True)

    def mix_values(mixture, h, slot):
        at = pl.multiple_of(mixture * MAXC, MAXC)
        exponent = jnp.exp2(scores[slot][h] - highest[slot][h : h + 1, :]).astype(BF)
        sums = dot(values_t[h, :, pl.ds(at, MAXC)], exponent)
        context_t[h * head : (h + 1) * head, pl.ds(at, MAXC)] = (
            sums[:head] / sums[head : head + 1]
        ).astype(BF)

    tall = wide * block
    for pos in range(PAIR):
        arrived(pos, recv_in, in_sems)

        def unpack(step, carry):
            start = pl.multiple_of(step * tall, tall)
            rows = blocks_of(recv_in, pos, step)
            slots_x[pl.ds(start, tall), :] = rows.astype(BF)
            slots_n[pl.ds(start, tall), :] = layer_norm(rows, gain_attn[...])
            return carry

        lax.fori_loop(0, steps, unpack, 0)

        def project(step, carry):
            start = pl.multiple_of(step * 2 * MAXC, 2 * MAXC)
            normed = dot(gather_m[pl.ds(start, 2 * MAXC), :], slots_n[...]).astype(BF)
            keys[pl.ds(start, 2 * MAXC), :] = dot(normed, w_key[...]).astype(BF)
            both = dot_nt(wqv_t[...], normed)
            query_t[:, pl.ds(start, 2 * MAXC)] = (both[:width] * scale).astype(BF)
            value = jnp.where(is_valid[:, pl.ds(start, 2 * MAXC)] > 0.0, both[width:], 0.0)
            value = value.astype(BF)
            for h in range(HEADS):
                values_t[h, 0:head, pl.ds(start, 2 * MAXC)] = value[h * head : (h + 1) * head]
            return carry

        lax.fori_loop(0, MIX // 2, project, 0)
        for h in range(HEADS):
            scores_of(0, h, 0)

        def attend(pair, carry):
            for slot in range(2):
                mixture = 2 * pair + slot
                for h in range(HEADS):
                    scores_of(mixture + 1, h, 1 - slot)
                    mix_values(mixture, h, slot)
            return carry

        lax.fori_loop(0, MIX // 2 - 1, attend, 0)
        for h in range(HEADS):
            scores_of(MIX - 1, h, 1)
            mix_values(MIX - 2, h, 0)
        for h in range(HEADS):
            mix_values(MIX - 1, h, 1)

        def combine(step, carry):
            start = pl.multiple_of(step * tall, tall)
            context = dot_nt(scatter_m[pl.ds(start, tall), :], context_t[...]).astype(BF)
            middle = slots_x[pl.ds(start, tall), :].astype(F32) + dot(context, w_out[...])
            middle = middle.astype(BF)
            for two in range(wide // 2):
                left = middle[2 * two * block : (2 * two + 1) * block]
                right = middle[(2 * two + 1) * block : (2 * two + 2) * block]
                rows = dot(repack_m[...], halves(left, right)).astype(BF)
                first = (step * (wide // 2) + two) * 2 * eight
                for side in range(2):
                    send_out[pos, pl.ds(first + side * eight, eight)] = rows[
                        :, side * LANES : (side + 1) * LANES
                    ].reshape(eight, 2 * groups, LANES)
            return carry

        lax.fori_loop(0, steps, combine, 0)
        exchange(pos, send_out, recv_out, out_sems)

    for pos in range(PAIR):
        arrived(pos, recv_out, out_sems)

        def finish(step, carry):
            start = pl.multiple_of(step * tall, tall)
            rows = blocks_of(recv_out, pos, step)
            second = layer_norm(rows, gain_ffn[...])
            hidden = jnp.maximum(dot(second, w_up[...]), 0.0).astype(BF)
            rows = (rows + dot(hidden, w_down[...])).astype(BF)
            if pos == 0:
                early[pl.ds(start, tall), :] = rows
            else:
                before = early[pl.ds(start, tall), :]
                for side in range(wide):
                    cut = slice(side * block, (side + 1) * block)
                    both = jnp.concatenate([before[cut], rows[cut]], axis=0)
                    both = dot(final_m[...], both).astype(BF)
                    place = pl.multiple_of((step * wide + side) * 2 * eight, 2 * eight)
                    result[:, pl.ds(place, 2 * eight), :] = both.reshape(
                        groups, 2 * eight, width
                    )
            return carry

        lax.fori_loop(0, steps, finish, 0)

    for pos in range(PAIR):
        sent(pos, send_in, in_sems)
        sent(pos, send_out, out_sems)


def local(
    axis_sizes,
    features,
    gain_attn,
    w_query,
    w_key,
    w_value,
    w_out,
    gain_ffn,
    w_up,
    w_down,
    counts,
    offsets,
):
    groups, positions, width = features.shape
    devices = axis_sizes[0] * axis_sizes[1]
    slots = groups * devices
    matrices = [jnp.asarray(m, BF) for m in permutations(groups, 8)]
    vmem = pl.BlockSpec(memory_space=pltpu.VMEM)
    smem = pl.BlockSpec(memory_space=pltpu.SMEM)
    link = pltpu.VMEM((PAIR, devices, 2 * groups, LANES), BF)
    return pl.pallas_call(
        functools.partial(kernel, (devices, axis_sizes)),
        out_shape=jax.ShapeDtypeStruct(features.shape, BF),
        in_specs=[smem, smem] + [vmem] * 13,
        out_specs=vmem,
        scratch_shapes=[
            link,
            link,
            link,
            link,
            pltpu.VMEM((slots, width), BF),
            pltpu.VMEM((slots, width), BF),
            pltpu.VMEM((MIX * MAXC, slots), BF),
            pltpu.VMEM((slots, MIX * MAXC), BF),
            pltpu.VMEM((width, MIX * MAXC), BF),
            pltpu.VMEM((2 * width, width), BF),
            pltpu.VMEM((1, MIX * MAXC), F32),
            pltpu.VMEM((width, MIX * MAXC), BF),
            pltpu.VMEM((MIX * MAXC, width), BF),
            pltpu.VMEM((HEADS, width // HEADS + 16, MIX * MAXC), BF),
            pltpu.VMEM((HEADS, MAXC, MAXC), F32),
            pltpu.VMEM((HEADS, MAXC, MAXC), F32),
            pltpu.VMEM((HEADS, MAXC), F32),
            pltpu.VMEM((HEADS, MAXC), F32),
            pltpu.VMEM((slots, width), BF),
            pltpu.SemaphoreType.DMA((3 * PAIR,)),
            pltpu.SemaphoreType.DMA((3 * PAIR,)),
        ],
        compiler_params=pltpu.CompilerParams(
            collective_id=0, has_side_effects=True, vmem_limit_bytes=56 << 20
        ),
    )(
        counts,
        offsets,
        features,
        gain_attn.reshape(1, width),
        w_query,
        w_key,
        w_value,
        w_out,
        gain_ffn.reshape(1, width),
        w_up,
        w_down,
        *matrices,
    )


def solution(mesh):
    axis_sizes = (mesh.shape["group"], mesh.shape["pos"])
    return jax.shard_map(
        functools.partial(local, axis_sizes),
        mesh=mesh,
        in_specs=(P(("group", "pos"), None, None),) + (P(),) * 10,
        out_specs=P(("group", "pos"), None, None),
        check_vma=False,
    )
```

```python
import functools
import math

import jax
import jax.numpy as jnp
import numpy as np
from jax import lax
from jax.experimental import pallas as pl
from jax.experimental.pallas import tpu as pltpu
from jax.sharding import PartitionSpec as P

HEADS = 8
MIX = 6
MAXC = 256
LANES = 128
PAIR = 2

epsilon = 1e-05
BF = jnp.bfloat16
F32 = jnp.float32
MESH = pl.DeviceIdType.MESH


def one_hot_rows(picks, width):
    matrix = np.zeros((len(picks), width), np.float32)
    matrix[np.arange(len(picks)), picks] = 1.0
    return matrix


def permutations(groups, eight):
    pack = [
        half * groups * 2 * eight + slot * 2 * eight + PAIR * device + pos
        for pos in range(PAIR)
        for device in range(eight)
        for half in range(2)
        for slot in range(groups)
    ]
    unpack = [
        device * 2 * groups + half * groups + slot
        for half in range(2)
        for device in range(eight)
        for slot in range(groups)
    ]
    final = [
        pos * eight * groups + device * groups + slot
        for slot in range(groups)
        for device in range(eight)
        for pos in range(PAIR)
    ]
    unpack_matrix = one_hot_rows(unpack, 2 * eight * groups)
    return (
        one_hot_rows(pack, 2 * 2 * eight * groups),
        unpack_matrix,
        unpack_matrix.T.copy(),
        one_hot_rows(final, PAIR * eight * groups),
    )


def dot(left, right):
    return jnp.dot(left, right, preferred_element_type=F32)


def dot_nt(left, right):
    return lax.dot_general(
        left, right, (((1,), (1,)), ((), ())), preferred_element_type=F32
    )


def layer_norm(floats, gain):
    average = jnp.mean(floats, axis=-1, keepdims=True)
    centred = floats - average
    spread = jnp.mean(centred * centred, axis=-1, keepdims=True)
    return (centred * lax.rsqrt(spread + epsilon) * gain).astype(BF)


def halves(left, right):
    low = jnp.concatenate([left[:, :LANES], right[:, :LANES]], axis=1)
    high = jnp.concatenate([left[:, LANES:], right[:, LANES:]], axis=1)
    return jnp.concatenate([low, high], axis=0)


def unhalves(rows):
    count = rows.shape[0] // 2
    left = jnp.concatenate([rows[:count, :LANES], rows[count:, :LANES]], axis=1)
    right = jnp.concatenate([rows[:count, LANES:], rows[count:, LANES:]], axis=1)
    return jnp.concatenate([left, right], axis=0)


def kernel(
    sizes,
    counts,
    offsets,
    features,
    gain_attn,
    w_query,
    w_key,
    w_value,
    w_out,
    gain_ffn,
    w_up,
    w_down,
    pack_m,
    unpack_m,
    repack_m,
    final_m,
    result,
    send_in,
    recv_in,
    send_out,
    recv_out,
    slots_x,
    slots_n,
    gather_m,
    scatter_m,
    context_t,
    wq_t,
    wv_t,
    is_valid,
    normed,
    query_t,
    keys,
    values_t,
    scores,
    highest,
    hidden,
    early,
    in_sems,
    out_sems,
):
    devices, axis_sizes = sizes
    groups = features.shape[0]
    width = features.shape[2]
    slots = devices * groups
    eight = 8
    block = eight * groups
    wide = 4
    steps = devices // (wide * eight)
    group_at = lax.axis_index("group")
    pos_at = lax.axis_index("pos")
    me = group_at * axis_sizes[1] + pos_at

    barrier = pltpu.get_barrier_semaphore()

    along = [lax.rem(pos_at + hop, axis_sizes[1]) for hop in range(axis_sizes[1])]

    def greet(group, place):
        pl.semaphore_signal(barrier, inc=1, device_id=(group, place), device_id_type=MESH)

    def greet_group(step, carry):
        for place in along:
            greet(lax.rem(group_at + step, axis_sizes[0]), place)
        return carry

    for place in along[1:]:
        greet(group_at, place)
    lax.fori_loop(1, axis_sizes[0], greet_group, 0)

    def pack(step, carry):
        start = pl.multiple_of(step * 4 * eight, 4 * eight)
        left = features[:, pl.ds(start, 2 * eight), :].reshape(2 * block, width)
        right = features[:, pl.ds(pl.multiple_of(start + 2 * eight, 2 * eight), 2 * eight), :]
        right = right.reshape(2 * block, width)
        rows = dot(pack_m[...], halves(left, right)).astype(BF)
        for pos in range(PAIR):
            part = rows[pos * 2 * block : (pos + 1) * 2 * block]
            for side in range(2):
                send_in[pos, pl.ds(step * 2 * eight + side * eight, eight)] = part[
                    :, side * LANES : (side + 1) * LANES
                ].reshape(eight, 2 * groups, LANES)
        return carry

    lax.fori_loop(0, devices // (2 * eight), pack, 0, unroll=2)
    pl.semaphore_wait(barrier, devices - 1)

    def exchange(pos, source, target, sems):
        own = pltpu.make_async_copy(
            source.at[pos, me], target.at[pos, me], sems.at[2 * PAIR + pos]
        )
        own.start()
        def send(group, place):
            pltpu.make_async_remote_copy(
                src_ref=source.at[pos, group * axis_sizes[1] + place],
                dst_ref=target.at[pos, me],
                send_sem=sems.at[pos],
                recv_sem=sems.at[PAIR + pos],
                device_id=(group, place),
                device_id_type=MESH,
            ).start()

        for place in along[1:]:
            send(group_at, place)

        def send_group(step, carry):
            group = lax.rem(group_at + step * 13, axis_sizes[0])
            for place in along:
                send(group, place)
            return carry

        lax.fori_loop(1, axis_sizes[0], send_group, 0)

    def arrived(pos, target, sems):
        others = target.at[pos, pl.ds(0, devices - 1)]
        pltpu.make_async_copy(others, others, sems.at[PAIR + pos]).wait()
        pltpu.make_async_copy(
            target.at[pos, me], target.at[pos, me], sems.at[2 * PAIR + pos]
        ).wait()

    def sent(pos, source, sems):
        others = source.at[pos, pl.ds(0, devices - 1)]
        pltpu.make_async_copy(others, others, sems.at[pos]).wait()

    for pos in range(PAIR):
        exchange(pos, send_in, recv_in, in_sems)

    def select_in(mixture, carry):
        row = lax.broadcasted_iota(jnp.int32, (MAXC, 1), 0)
        pick = jnp.where(row < counts[mixture], row, 0) + offsets[mixture]
        column = lax.broadcasted_iota(jnp.int32, (MAXC, slots), 1)
        gather_m[pl.ds(pl.multiple_of(mixture * MAXC, MAXC), MAXC), :] = jnp.where(column == pick, 1.0, 0.0).astype(BF)
        return carry

    lax.fori_loop(0, MIX, select_in, 0)

    def select_out(step, carry):
        start = pl.multiple_of(step * 2 * block, 2 * block)
        slot = start + lax.broadcasted_iota(jnp.int32, (2 * block, 1), 0)
        pick = jnp.full((2 * block, 1), -1, jnp.int32)
        for mixture in range(MIX):
            place = slot - offsets[mixture]
            inside = (place >= 0) & (place < counts[mixture])
            pick = jnp.where(inside, place + mixture * MAXC, pick)
        column = lax.broadcasted_iota(jnp.int32, (2 * block, MIX * MAXC), 1)
        scatter_m[pl.ds(start, 2 * block), :] = jnp.where(column == pick, 1.0, 0.0).astype(BF)
        return carry

    lax.fori_loop(0, devices // (2 * eight), select_out, 0)
    head = width // HEADS
    scale = math.log2(math.e) / math.sqrt(head)
    wq_t[...] = w_query[...].astype(F32).T.astype(BF)
    wv_t[...] = w_value[...].astype(F32).T.astype(BF)
    column = lax.broadcasted_iota(jnp.int32, (1, MIX * MAXC), 1)
    valid = jnp.zeros((1, MIX * MAXC), F32)
    for mixture in range(MIX):
        inside = (column >= mixture * MAXC) & (column < mixture * MAXC + counts[mixture])
        valid = jnp.where(inside, 1.0, valid)
    is_valid[...] = valid

    def two_blocks(buffer, pos, step):
        rows = []
        for two in range(wide // 2):
            first = (step * (wide // 2) + two) * 2 * eight
            sides = [
                buffer[pos, pl.ds(first + side * eight, eight)].reshape(2 * block, LANES)
                for side in range(2)
            ]
            rows.append(unhalves(dot(unpack_m[...], jnp.concatenate(sides, axis=1))))
        return rows

    def project_keys(mixture, to):
        at = pl.multiple_of(mixture * MAXC, MAXC)
        chosen = normed[pl.ds(at, MAXC), :]
        keys[to][...] = dot(chosen, w_key[...]).astype(BF)
        query_t[to][...] = (dot_nt(wq_t[...], chosen) * scale).astype(BF)

    def project_values(mixture, to):
        at = pl.multiple_of(mixture * MAXC, MAXC)
        valid = is_valid[:, pl.ds(at, MAXC)]
        value = jnp.where(valid > 0.0, dot_nt(wv_t[...], normed[pl.ds(at, MAXC), :]), 0.0).astype(BF)
        ones = jnp.broadcast_to(valid, (16, MAXC)).astype(BF)
        for h in range(HEADS):
            values_t[to][h, 0:head, :] = value[h * head : (h + 1) * head]
            values_t[to][h, head:, :] = ones

    def scores_of(h, to):
        lane_head = lax.broadcasted_iota(jnp.int32, (1, width), 1) // head
        mask = jnp.where(lane_head == h, 1.0, 0.0).astype(BF)
        logits = dot(keys[to][...] * mask, query_t[to][...])
        scores[to][h] = logits
        highest[to][h : h + 1, :] = jnp.max(logits, axis=0, keepdims=True)

    def mix_values(mixture, h, to):
        at = pl.multiple_of(mixture * MAXC, MAXC)
        exponent = jnp.exp2(scores[to][h] - highest[to][h : h + 1, :]).astype(BF)
        sums = dot(values_t[to][h], exponent)
        context_t[h * head : (h + 1) * head, pl.ds(at, MAXC)] = (
            sums[:head] / sums[head : head + 1]
        ).astype(BF)

    tall = wide * block
    for pos in range(PAIR):
        arrived(pos, recv_in, in_sems)

        def unpack(step, carry):
            start = pl.multiple_of(step * tall, tall)
            for two, rows in enumerate(two_blocks(recv_in, pos, step)):
                at = pl.multiple_of(start + two * 2 * block, 2 * block)
                slots_x[pl.ds(at, 2 * block), :] = rows.astype(BF)
                slots_n[pl.ds(at, 2 * block), :] = layer_norm(rows, gain_attn[...])
            return carry

        lax.fori_loop(0, steps, unpack, 0, unroll=2)

        def gather(pair, carry):
            places = [
                pl.multiple_of((2 * pair + two) * MAXC, MAXC) for two in range(2)
            ]
            chosen = [dot(gather_m[pl.ds(at, MAXC), :], slots_n[...]) for at in places]
            for at, rows in zip(places, chosen):
                normed[pl.ds(at, MAXC), :] = rows.astype(BF)
            return carry

        lax.fori_loop(0, MIX // 2, gather, 0)
        project_keys(0, 0)
        project_keys(1, 1)
        project_values(0, 0)
        for h in range(HEADS):
            scores_of(h, 0)

        def attend(pair, carry):
            for to in range(2):
                mixture = 2 * pair + to
                for h in range(HEADS):
                    scores_of(h, 1 - to)
                    mix_values(mixture, h, to)
                    if h == 1:
                        project_values(mixture + 1, 1 - to)
                    if h == 4:
                        project_keys(mixture + 2, to)
            return carry

        lax.fori_loop(0, MIX // 2 - 1, attend, 0)
        project_values(MIX - 1, 1)
        for h in range(HEADS):
            scores_of(h, 1)
            mix_values(MIX - 2, h, 0)
        for h in range(HEADS):
            mix_values(MIX - 1, h, 1)

        def combine(step, carry):
            twos = range(wide // 2)
            starts = [
                pl.multiple_of((step * (wide // 2) + two) * 2 * block, 2 * block) for two in twos
            ]
            rows = [
                dot_nt(scatter_m[pl.ds(start, 2 * block), :], context_t[...]).astype(BF)
                for start in starts
            ]
            rows = [dot(row, w_out[...]) for row in rows]
            rows = [
                (row + slots_x[pl.ds(start, 2 * block), :].astype(F32)).astype(BF)
                for row, start in zip(rows, starts)
            ]
            rows = [dot(repack_m[...], halves(row[:block], row[block:])).astype(BF) for row in rows]
            for two in twos:
                first = (step * (wide // 2) + two) * 2 * eight
                for side in range(2):
                    send_out[pos, pl.ds(first + side * eight, eight)] = rows[two][
                        :, side * LANES : (side + 1) * LANES
                    ].reshape(eight, 2 * groups, LANES)
            return carry

        lax.fori_loop(0, steps, combine, 0)
        exchange(pos, send_out, recv_out, out_sems)

    for pos in range(PAIR):
        arrived(pos, recv_out, out_sems)

        def finish(step, carry):
            twos = range(wide // 2)
            starts = [
                pl.multiple_of((step * (wide // 2) + two) * 2 * block, 2 * block) for two in twos
            ]
            rows = two_blocks(recv_out, pos, step)
            second = [layer_norm(row, gain_ffn[...]) for row in rows]
            for cut in range(0, w_up.shape[1], width):
                for two in twos:
                    hidden[two][:, cut : cut + width] = jnp.maximum(
                        dot(second[two], w_up[:, cut : cut + width]), 0.0
                    ).astype(BF)
            rows = [(rows[two] + dot(hidden[two][...], w_down[...])).astype(BF) for two in twos]
            if pos == 0:
                for two in twos:
                    early[pl.ds(starts[two], 2 * block), :] = rows[two]
            else:
                for two in twos:
                    before = early[pl.ds(starts[two], 2 * block), :]
                    for side in range(2):
                        cut = slice(side * block, (side + 1) * block)
                        both = jnp.concatenate([before[cut], rows[two][cut]], axis=0)
                        both = dot(final_m[...], both).astype(BF)
                        place = (step * wide + 2 * two + side) * 2 * eight
                        place = pl.multiple_of(place, 2 * eight)
                        result[:, pl.ds(place, 2 * eight), :] = both.reshape(
                            groups, 2 * eight, width
                        )
            return carry

        lax.fori_loop(0, steps, finish, 0)

    for pos in range(PAIR):
        sent(pos, send_in, in_sems)
        sent(pos, send_out, out_sems)


def local(
    axis_sizes,
    features,
    gain_attn,
    w_query,
    w_key,
    w_value,
    w_out,
    gain_ffn,
    w_up,
    w_down,
    counts,
    offsets,
):
    groups, positions, width = features.shape
    devices = axis_sizes[0] * axis_sizes[1]
    slots = groups * devices
    matrices = [jnp.asarray(m, BF) for m in permutations(groups, 8)]
    vmem = pl.BlockSpec(memory_space=pltpu.VMEM)
    smem = pl.BlockSpec(memory_space=pltpu.SMEM)
    link = pltpu.VMEM((PAIR, devices, 2 * groups, LANES), BF)

    def both(shape):
        return (shape, shape)

    return pl.pallas_call(
        functools.partial(kernel, (devices, axis_sizes)),
        out_shape=jax.ShapeDtypeStruct(features.shape, BF),
        in_specs=[smem, smem] + [vmem] * 13,
        out_specs=vmem,
        scratch_shapes=[
            link,
            link,
            link,
            link,
            pltpu.VMEM((slots, width), BF),
            pltpu.VMEM((slots, width), BF),
            pltpu.VMEM((MIX * MAXC, slots), BF),
            pltpu.VMEM((slots, MIX * MAXC), BF),
            pltpu.VMEM((width, MIX * MAXC), BF),
            pltpu.VMEM((width, width), BF),
            pltpu.VMEM((width, width), BF),
            pltpu.VMEM((1, MIX * MAXC), F32),
            pltpu.VMEM((MIX * MAXC, width), BF),
            both(pltpu.VMEM((width, MAXC), BF)),
            both(pltpu.VMEM((MAXC, width), BF)),
            both(pltpu.VMEM((HEADS, width // HEADS + 16, MAXC), BF)),
            both(pltpu.VMEM((HEADS, MAXC, MAXC), F32)),
            both(pltpu.VMEM((HEADS, MAXC), F32)),
            both(pltpu.VMEM((16 * groups, w_up.shape[1]), BF)),
            pltpu.VMEM((slots, width), BF),
            pltpu.SemaphoreType.DMA((3 * PAIR,)),
            pltpu.SemaphoreType.DMA((3 * PAIR,)),
        ],
        compiler_params=pltpu.CompilerParams(
            collective_id=0, has_side_effects=True, vmem_limit_bytes=56 << 20
        ),
    )(
        counts,
        offsets,
        features,
        gain_attn.reshape(1, width),
        w_query,
        w_key,
        w_value,
        w_out,
        gain_ffn.reshape(1, width),
        w_up,
        w_down,
        *matrices,
    )


def solution(mesh):
    axis_sizes = (mesh.shape["group"], mesh.shape["pos"])
    return jax.shard_map(
        functools.partial(local, axis_sizes),
        mesh=mesh,
        in_specs=(P(("group", "pos"), None, None),) + (P(),) * 10,
        out_specs=P(("group", "pos"), None, None),
        check_vma=False,
    )
```

```python
import functools
import math

import jax
import jax.numpy as jnp
import numpy as np
from jax import lax
from jax.experimental import pallas as pl
from jax.experimental.pallas import tpu as pltpu
from jax.sharding import PartitionSpec as P

HEADS = 8
MIX = 6
MAXC = 256
LANES = 128
PAIR = 2
PLANES = 4

epsilon = 1e-05
BF = jnp.bfloat16
F32 = jnp.float32
MESH = pl.DeviceIdType.MESH


def one_hot_rows(picks, width):
    matrix = np.zeros((len(picks), width), np.float32)
    matrix[np.arange(len(picks)), picks] = 1.0
    return matrix


def permutations(groups, eight):
    pack = [
        half * groups * 2 * eight + slot * 2 * eight + PAIR * device + pos
        for pos in range(PAIR)
        for device in range(eight)
        for half in range(2)
        for slot in range(groups)
    ]
    unpack = [
        device * 2 * groups + half * groups + slot
        for half in range(2)
        for device in range(eight)
        for slot in range(groups)
    ]
    final = [
        pos * eight * groups + device * groups + slot
        for slot in range(groups)
        for device in range(eight)
        for pos in range(PAIR)
    ]
    unpack_matrix = one_hot_rows(unpack, 2 * eight * groups)
    return (
        one_hot_rows(pack, 2 * 2 * eight * groups),
        unpack_matrix,
        unpack_matrix.T.copy(),
        one_hot_rows(final, PAIR * eight * groups),
    )


def dot(left, right):
    return jnp.dot(left, right, preferred_element_type=F32)


def dot_nt(left, right):
    return lax.dot_general(
        left, right, (((1,), (1,)), ((), ())), preferred_element_type=F32
    )


def layer_norm(floats, gain):
    average = jnp.mean(floats, axis=-1, keepdims=True)
    centred = floats - average
    spread = jnp.mean(centred * centred, axis=-1, keepdims=True)
    return (centred * lax.rsqrt(spread + epsilon) * gain).astype(BF)


def halves(left, right):
    low = jnp.concatenate([left[:, :LANES], right[:, :LANES]], axis=1)
    high = jnp.concatenate([left[:, LANES:], right[:, LANES:]], axis=1)
    return jnp.concatenate([low, high], axis=0)


def unhalves(rows):
    count = rows.shape[0] // 2
    left = jnp.concatenate([rows[:count, :LANES], rows[count:, :LANES]], axis=1)
    right = jnp.concatenate([rows[:count, LANES:], rows[count:, LANES:]], axis=1)
    return jnp.concatenate([left, right], axis=0)


def kernel(
    sizes,
    counts,
    offsets,
    *refs,
):
    operands, (result, staged, load_sems), rest = refs[:13], refs[13:16], refs[16:]
    (
        features,
        gain_attn,
        w_query,
        w_key,
        w_value,
        w_out,
        gain_ffn,
        w_up,
        w_down,
        pack_m,
        unpack_m,
        repack_m,
        final_m,
    ) = staged
    (
        send_in,
        recv_in,
        send_out,
        recv_out,
        slots_x,
        slots_n,
        gather_m,
        scatter_m,
        context_t,
        wq_t,
        wv_t,
        is_valid,
        normed,
        query_t,
        keys,
        values_t,
        scores,
        highest,
        hidden,
        early,
        in_sems,
        out_sems,
        own_in,
        own_out,
    ) = rest
    devices, axis_sizes = sizes
    groups = features.shape[0]
    width = features.shape[2]
    slots = devices * groups
    eight = 8
    block = eight * groups
    wide = 4
    assert devices == PLANES * wide * eight
    group_at = lax.axis_index("group")
    pos_at = lax.axis_index("pos")
    me = group_at * axis_sizes[1] + pos_at
    per_plane = axis_sizes[0] // PLANES
    plane_at = group_at // per_plane
    inner_at = lax.rem(group_at, per_plane)

    loads = [
        pltpu.make_async_copy(operand, place, load_sems.at[at])
        for at, (operand, place) in enumerate(zip(operands, staged))
    ]
    first_needed = (0, 9)
    for at in first_needed:
        loads[at].start()
    barrier = pltpu.get_barrier_semaphore()

    along = [lax.rem(pos_at + hop, axis_sizes[1]) for hop in range(axis_sizes[1])]

    def greet(group, place):
        pl.semaphore_signal(barrier, inc=1, device_id=(group, place), device_id_type=MESH)

    def greet_group(step, carry):
        for place in along:
            greet(lax.rem(group_at + step, axis_sizes[0]), place)
        return carry

    for place in along[1:]:
        greet(group_at, place)
    lax.fori_loop(1, axis_sizes[0], greet_group, 0)

    for at in range(len(loads)):
        if at not in first_needed:
            loads[at].start()
    for at in first_needed:
        loads[at].wait()

    def pack(step, carry):
        start = pl.multiple_of(step * 4 * eight, 4 * eight)
        left = features[:, pl.ds(start, 2 * eight), :].reshape(2 * block, width)
        right = features[:, pl.ds(pl.multiple_of(start + 2 * eight, 2 * eight), 2 * eight), :]
        right = right.reshape(2 * block, width)
        rows = dot(pack_m[...], halves(left, right)).astype(BF)
        for pos in range(PAIR):
            part = rows[pos * 2 * block : (pos + 1) * 2 * block]
            for side in range(2):
                send_in[pos, pl.ds(step * 2 * eight + side * eight, eight)] = part[
                    :, side * LANES : (side + 1) * LANES
                ].reshape(eight, 2 * groups, LANES)
        return carry

    lax.fori_loop(0, devices // (2 * eight), pack, 0, unroll=2)
    pl.semaphore_wait(barrier, devices - 1)

    def exchange(pos, phase, source, target, sems, own_sems):
        planes = [lax.rem(plane_at + phase + 2 * two, PLANES) for two in range(2)]
        if phase == 0:
            pltpu.make_async_copy(
                source.at[pos, me], target.at[pos, me], own_sems.at[pos]
            ).start()

        def send(group, place):
            pltpu.make_async_remote_copy(
                src_ref=source.at[pos, group * axis_sizes[1] + place],
                dst_ref=target.at[pos, me],
                send_sem=sems.at[pos, phase, 0],
                recv_sem=sems.at[pos, phase, 1],
                device_id=(group, place),
                device_id_type=MESH,
            ).start()

        def send_group(step, carry):
            inner = lax.rem(inner_at + step, per_plane)
            for place in along:
                for plane in planes:
                    send(plane * per_plane + inner, place)
            return carry

        if phase == 0:
            for place in along:
                send(planes[1] * per_plane + inner_at, place)
            for place in along[1:]:
                send(group_at, place)
        lax.fori_loop(1 - phase, per_plane, send_group, 0)

    def blocks_in(phase):
        return devices // 2 - (1 if phase == 0 else 0)

    def arrived(pos, phase, target, sems, own_sems):
        others = target.at[pos, pl.ds(0, blocks_in(phase))]
        pltpu.make_async_copy(others, others, sems.at[pos, phase, 1]).wait()
        if phase == 0:
            own = target.at[pos, me]
            pltpu.make_async_copy(own, own, own_sems.at[pos]).wait()

    def sent(pos, source, sems):
        for phase in range(2):
            others = source.at[pos, pl.ds(0, blocks_in(phase))]
            pltpu.make_async_copy(others, others, sems.at[pos, phase, 0]).wait()

    def near(phase, step):
        return lax.rem(plane_at + phase + 2 * step, PLANES)

    for pos in range(PAIR):
        for phase in range(2):
            exchange(pos, phase, send_in, recv_in, in_sems, own_in)

    for at in range(len(loads)):
        if at not in first_needed:
            loads[at].wait()

    def select_in(mixture, carry):
        row = lax.broadcasted_iota(jnp.int32, (MAXC, 1), 0)
        pick = jnp.where(row < counts[mixture], row, 0) + offsets[mixture]
        column = lax.broadcasted_iota(jnp.int32, (MAXC, slots), 1)
        gather_m[pl.ds(pl.multiple_of(mixture * MAXC, MAXC), MAXC), :] = jnp.where(column == pick, 1.0, 0.0).astype(BF)
        return carry

    lax.fori_loop(0, MIX, select_in, 0)

    def select_out(step, carry):
        start = pl.multiple_of(step * 2 * block, 2 * block)
        slot = start + lax.broadcasted_iota(jnp.int32, (2 * block, 1), 0)
        pick = jnp.full((2 * block, 1), -1, jnp.int32)
        for mixture in range(MIX):
            place = slot - offsets[mixture]
            inside = (place >= 0) & (place < counts[mixture])
            pick = jnp.where(inside, place + mixture * MAXC, pick)
        column = lax.broadcasted_iota(jnp.int32, (2 * block, MIX * MAXC), 1)
        scatter_m[pl.ds(start, 2 * block), :] = jnp.where(column == pick, 1.0, 0.0).astype(BF)
        return carry

    lax.fori_loop(0, devices // (2 * eight), select_out, 0)
    head = width // HEADS
    scale = math.log2(math.e) / math.sqrt(head)
    wq_t[...] = w_query[...].astype(F32).T.astype(BF)
    wv_t[...] = w_value[...].astype(F32).T.astype(BF)
    column = lax.broadcasted_iota(jnp.int32, (1, MIX * MAXC), 1)
    valid = jnp.zeros((1, MIX * MAXC), F32)
    for mixture in range(MIX):
        inside = (column >= mixture * MAXC) & (column < mixture * MAXC + counts[mixture])
        valid = jnp.where(inside, 1.0, valid)
    is_valid[...] = valid

    def two_blocks(buffer, pos, step):
        rows = []
        for two in range(wide // 2):
            first = (step * (wide // 2) + two) * 2 * eight
            sides = [
                buffer[pos, pl.ds(first + side * eight, eight)].reshape(2 * block, LANES)
                for side in range(2)
            ]
            rows.append(unhalves(dot(unpack_m[...], jnp.concatenate(sides, axis=1))))
        return rows

    def project_keys(mixture, to):
        at = pl.multiple_of(mixture * MAXC, MAXC)
        chosen = normed[pl.ds(at, MAXC), :]
        keys[to][...] = dot(chosen, w_key[...]).astype(BF)
        query_t[to][...] = (dot_nt(wq_t[...], chosen) * scale).astype(BF)

    def project_values(mixture, to):
        at = pl.multiple_of(mixture * MAXC, MAXC)
        valid = is_valid[:, pl.ds(at, MAXC)]
        value = jnp.where(valid > 0.0, dot_nt(wv_t[...], normed[pl.ds(at, MAXC), :]), 0.0).astype(BF)
        ones = jnp.broadcast_to(valid, (16, MAXC)).astype(BF)
        for h in range(HEADS):
            values_t[to][h, 0:head, :] = value[h * head : (h + 1) * head]
            values_t[to][h, head:, :] = ones

    def scores_of(h, to):
        lane_head = lax.broadcasted_iota(jnp.int32, (1, width), 1) // head
        mask = jnp.where(lane_head == h, 1.0, 0.0).astype(BF)
        logits = dot(keys[to][...] * mask, query_t[to][...])
        scores[to][h] = logits
        highest[to][h : h + 1, :] = jnp.max(logits, axis=0, keepdims=True)

    def mix_values(mixture, h, to):
        at = pl.multiple_of(mixture * MAXC, MAXC)
        exponent = jnp.exp2(scores[to][h] - highest[to][h : h + 1, :]).astype(BF)
        sums = dot(values_t[to][h], exponent)
        context_t[h * head : (h + 1) * head, pl.ds(at, MAXC)] = (
            sums[:head] / sums[head : head + 1]
        ).astype(BF)

    tall = wide * block
    for pos in range(PAIR):
        def unpack(phase, step, carry):
            step = near(phase, step)
            start = pl.multiple_of(step * tall, tall)
            for two, rows in enumerate(two_blocks(recv_in, pos, step)):
                at = pl.multiple_of(start + two * 2 * block, 2 * block)
                slots_x[pl.ds(at, 2 * block), :] = rows.astype(BF)
                slots_n[pl.ds(at, 2 * block), :] = layer_norm(rows, gain_attn[...])
            return carry

        for phase in range(2):
            arrived(pos, phase, recv_in, in_sems, own_in)
            lax.fori_loop(0, 2, functools.partial(unpack, phase), 0, unroll=2)

        def gather(pair, carry):
            places = [
                pl.multiple_of((2 * pair + two) * MAXC, MAXC) for two in range(2)
            ]
            chosen = [dot(gather_m[pl.ds(at, MAXC), :], slots_n[...]) for at in places]
            for at, rows in zip(places, chosen):
                normed[pl.ds(at, MAXC), :] = rows.astype(BF)
            return carry

        lax.fori_loop(0, MIX // 2, gather, 0)
        project_keys(0, 0)
        project_keys(1, 1)
        project_values(0, 0)
        for h in range(HEADS):
            scores_of(h, 0)

        def attend(pair, carry):
            for to in range(2):
                mixture = 2 * pair + to
                for h in range(HEADS):
                    scores_of(h, 1 - to)
                    mix_values(mixture, h, to)
                    if h == 1:
                        project_values(mixture + 1, 1 - to)
                    if h == 4:
                        project_keys(mixture + 2, to)
            return carry

        lax.fori_loop(0, MIX // 2 - 1, attend, 0)
        project_values(MIX - 1, 1)
        for h in range(HEADS):
            scores_of(h, 1)
            mix_values(MIX - 2, h, 0)
        for h in range(HEADS):
            mix_values(MIX - 1, h, 1)

        def combine(phase, step, carry):
            step = near(phase, step)
            twos = range(wide // 2)
            starts = [
                pl.multiple_of((step * (wide // 2) + two) * 2 * block, 2 * block) for two in twos
            ]
            rows = [
                dot_nt(scatter_m[pl.ds(start, 2 * block), :], context_t[...]).astype(BF)
                for start in starts
            ]
            rows = [dot(row, w_out[...]) for row in rows]
            rows = [
                (row + slots_x[pl.ds(start, 2 * block), :].astype(F32)).astype(BF)
                for row, start in zip(rows, starts)
            ]
            rows = [dot(repack_m[...], halves(row[:block], row[block:])).astype(BF) for row in rows]
            for two in twos:
                first = (step * (wide // 2) + two) * 2 * eight
                for side in range(2):
                    send_out[pos, pl.ds(first + side * eight, eight)] = rows[two][
                        :, side * LANES : (side + 1) * LANES
                    ].reshape(eight, 2 * groups, LANES)
            return carry

        for phase in range(2):
            lax.fori_loop(0, 2, functools.partial(combine, phase), 0)
            exchange(pos, phase, send_out, recv_out, out_sems, own_out)

    for pos in range(PAIR):
        def finish(phase, step, carry):
            step = near(phase, step)
            twos = range(wide // 2)
            starts = [
                pl.multiple_of((step * (wide // 2) + two) * 2 * block, 2 * block) for two in twos
            ]
            rows = two_blocks(recv_out, pos, step)
            second = [layer_norm(row, gain_ffn[...]) for row in rows]
            for cut in range(0, w_up.shape[1], width):
                for two in twos:
                    hidden[two][:, cut : cut + width] = jnp.maximum(
                        dot(second[two], w_up[:, cut : cut + width]), 0.0
                    ).astype(BF)
            rows = [(rows[two] + dot(hidden[two][...], w_down[...])).astype(BF) for two in twos]
            if pos == 0:
                for two in twos:
                    early[pl.ds(starts[two], 2 * block), :] = rows[two]
            else:
                for two in twos:
                    before = early[pl.ds(starts[two], 2 * block), :]
                    for side in range(2):
                        cut = slice(side * block, (side + 1) * block)
                        both = jnp.concatenate([before[cut], rows[two][cut]], axis=0)
                        both = dot(final_m[...], both).astype(BF)
                        place = (step * wide + 2 * two + side) * 2 * eight
                        place = pl.multiple_of(place, 2 * eight)
                        result[:, pl.ds(place, 2 * eight), :] = both.reshape(
                            groups, 2 * eight, width
                        )
            return carry

        for phase in range(2):
            arrived(pos, phase, recv_out, out_sems, own_out)
            lax.fori_loop(0, 2, functools.partial(finish, phase), 0)

    for pos in range(PAIR):
        sent(pos, send_in, in_sems)
        sent(pos, send_out, out_sems)


def local(
    axis_sizes,
    features,
    gain_attn,
    w_query,
    w_key,
    w_value,
    w_out,
    gain_ffn,
    w_up,
    w_down,
    counts,
    offsets,
):
    groups, positions, width = features.shape
    devices = axis_sizes[0] * axis_sizes[1]
    slots = groups * devices
    matrices = [jnp.asarray(m, BF) for m in permutations(groups, 8)]
    vmem = pl.BlockSpec(memory_space=pltpu.VMEM)
    smem = pl.BlockSpec(memory_space=pltpu.SMEM)
    link = pltpu.VMEM((PAIR, devices, 2 * groups, LANES), BF)

    def both(shape):
        return (shape, shape)

    operands = [
        features,
        gain_attn.reshape(1, width),
        w_query,
        w_key,
        w_value,
        w_out,
        gain_ffn.reshape(1, width),
        w_up,
        w_down,
        *matrices,
    ]

    return pl.pallas_call(
        functools.partial(kernel, (devices, axis_sizes)),
        out_shape=jax.ShapeDtypeStruct(features.shape, BF),
        in_specs=[smem, smem] + [pl.BlockSpec(memory_space=pl.ANY)] * 13,
        out_specs=vmem,
        scratch_shapes=[
            tuple(pltpu.VMEM(operand.shape, operand.dtype) for operand in operands),
            pltpu.SemaphoreType.DMA((len(operands),)),
            link,
            link,
            link,
            link,
            pltpu.VMEM((slots, width), BF),
            pltpu.VMEM((slots, width), BF),
            pltpu.VMEM((MIX * MAXC, slots), BF),
            pltpu.VMEM((slots, MIX * MAXC), BF),
            pltpu.VMEM((width, MIX * MAXC), BF),
            pltpu.VMEM((width, width), BF),
            pltpu.VMEM((width, width), BF),
            pltpu.VMEM((1, MIX * MAXC), F32),
            pltpu.VMEM((MIX * MAXC, width), BF),
            both(pltpu.VMEM((width, MAXC), BF)),
            both(pltpu.VMEM((MAXC, width), BF)),
            both(pltpu.VMEM((HEADS, width // HEADS + 16, MAXC), BF)),
            both(pltpu.VMEM((HEADS, MAXC, MAXC), F32)),
            both(pltpu.VMEM((HEADS, MAXC), F32)),
            both(pltpu.VMEM((16 * groups, w_up.shape[1]), BF)),
            pltpu.VMEM((slots, width), BF),
            pltpu.SemaphoreType.DMA((PAIR, 2, 2)),
            pltpu.SemaphoreType.DMA((PAIR, 2, 2)),
            pltpu.SemaphoreType.DMA((PAIR,)),
            pltpu.SemaphoreType.DMA((PAIR,)),
        ],
        compiler_params=pltpu.CompilerParams(
            collective_id=0, has_side_effects=True, vmem_limit_bytes=56 << 20
        ),
    )(counts, offsets, *operands)


def solution(mesh):
    axis_sizes = (mesh.shape["group"], mesh.shape["pos"])
    return jax.shard_map(
        functools.partial(local, axis_sizes),
        mesh=mesh,
        in_specs=(P(("group", "pos"), None, None),) + (P(),) * 10,
        out_specs=P(("group", "pos"), None, None),
        check_vma=False,
    )
```

```python
import functools
import math

import jax
import jax.numpy as jnp
import numpy as np
from jax import lax
from jax.experimental import pallas as pl
from jax.experimental.pallas import tpu as pltpu
from jax.sharding import PartitionSpec as P

HEADS = 8
MIX = 6
MAXC = 256
LANES = 128
PAIR = 2
SIDE = 4
PHASES = 4

epsilon = 1e-05
BF = jnp.bfloat16
F32 = jnp.float32
MESH = pl.DeviceIdType.MESH


def one_hot_rows(picks, width):
    matrix = np.zeros((len(picks), width), np.float32)
    matrix[np.arange(len(picks)), picks] = 1.0
    return matrix


def permutations(groups, eight):
    pack = [
        half * groups * 2 * eight + slot * 2 * eight + PAIR * device + pos
        for pos in range(PAIR)
        for device in range(eight)
        for half in range(2)
        for slot in range(groups)
    ]
    unpack = [
        device * 2 * groups + half * groups + slot
        for half in range(2)
        for device in range(eight)
        for slot in range(groups)
    ]
    final = [
        pos * eight * groups + device * groups + slot
        for slot in range(groups)
        for device in range(eight)
        for pos in range(PAIR)
    ]
    unpack_matrix = one_hot_rows(unpack, 2 * eight * groups)
    return (
        one_hot_rows(pack, 2 * 2 * eight * groups),
        unpack_matrix,
        unpack_matrix.T.copy(),
        one_hot_rows(final, PAIR * eight * groups),
    )


def dot(left, right):
    return jnp.dot(left, right, preferred_element_type=F32)


def dot_nt(left, right):
    return lax.dot_general(
        left, right, (((1,), (1,)), ((), ())), preferred_element_type=F32
    )


def layer_norm(floats, gain):
    average = jnp.mean(floats, axis=-1, keepdims=True)
    centred = floats - average
    spread = jnp.mean(centred * centred, axis=-1, keepdims=True)
    return (centred * lax.rsqrt(spread + epsilon) * gain).astype(BF)


def halves(left, right):
    low = jnp.concatenate([left[:, :LANES], right[:, :LANES]], axis=1)
    high = jnp.concatenate([left[:, LANES:], right[:, LANES:]], axis=1)
    return jnp.concatenate([low, high], axis=0)


def unhalves(rows):
    count = rows.shape[0] // 2
    left = jnp.concatenate([rows[:count, :LANES], rows[count:, :LANES]], axis=1)
    right = jnp.concatenate([rows[:count, LANES:], rows[count:, LANES:]], axis=1)
    return jnp.concatenate([left, right], axis=0)


def kernel(
    sizes,
    counts,
    offsets,
    *refs,
):
    operands, (result, finished, staged, load_sems, done), rest = refs[:13], refs[13:18], refs[18:]
    (
        features,
        gain_attn,
        w_query,
        w_key,
        w_value,
        w_out,
        gain_ffn,
        w_up,
        w_down,
        pack_m,
        unpack_m,
        repack_m,
        final_m,
    ) = staged
    (
        send_in,
        recv_in,
        send_out,
        recv_out,
        slots_x,
        slots_n,
        gather_m,
        scatter_m,
        context_t,
        wq_t,
        wv_t,
        is_valid,
        normed,
        query_t,
        keys,
        values_t,
        scores,
        highest,
        hidden,
        early,
        in_sems,
        out_sems,
        own_in,
        own_out,
    ) = rest
    devices, axis_sizes = sizes
    groups = features.shape[0]
    width = features.shape[2]
    slots = devices * groups
    eight = 8
    block = eight * groups
    wide = 4
    twos = range(wide // 2)
    assert devices == PHASES * wide * eight
    group_at = lax.axis_index("group")
    pos_at = lax.axis_index("pos")
    me = group_at * axis_sizes[1] + pos_at
    cores = axis_sizes[0] // (SIDE * SIDE)
    y_at = group_at // (SIDE * cores)
    x_at = lax.rem(group_at // cores, SIDE)
    core_at = lax.rem(group_at, cores)

    loads = [
        pltpu.make_async_copy(operand, place, load_sems.at[at])
        for at, (operand, place) in enumerate(zip(operands, staged))
    ]
    first_needed = (0, 9)
    for at in first_needed:
        loads[at].start()
    barrier = pltpu.get_barrier_semaphore()

    along = [lax.rem(pos_at + hop, axis_sizes[1]) for hop in range(axis_sizes[1])]

    def greet(group, place):
        pl.semaphore_signal(barrier, inc=1, device_id=(group, place), device_id_type=MESH)

    def greet_group(step, carry):
        for place in along:
            greet(lax.rem(group_at + step, axis_sizes[0]), place)
        return carry

    for place in along[1:]:
        greet(group_at, place)
    lax.fori_loop(1, axis_sizes[0], greet_group, 0)

    for at in range(len(loads)):
        if at not in first_needed:
            loads[at].start()
    for at in first_needed:
        loads[at].wait()

    def near(phase, at):
        y = lax.rem(y_at + phase // 2 + 2 * (at // 2), SIDE)
        x = lax.rem(x_at + phase % 2 + 2 * (at % 2), SIDE)
        return y * SIDE + x

    def in_phases(body):
        body(0, True)

        def later(phase, carry):
            body(phase, False)
            return carry

        lax.fori_loop(1, PHASES, later, 0)

    def exchange(pos, phase, first, source, target, sems, own_sems):
        def send_column(at, skip):
            column = near(phase, at)
            for core in range(cores):
                for hop in range(axis_sizes[1]):
                    if skip and core == 0 and hop == 0:
                        continue
                    group = column * cores + lax.rem(core_at + core, cores)
                    place = along[hop]
                    pltpu.make_async_remote_copy(
                        src_ref=source.at[pos, group * axis_sizes[1] + place],
                        dst_ref=target.at[pos, me],
                        send_sem=sems.at[pos, phase, 0],
                        recv_sem=sems.at[pos, phase, 1],
                        device_id=(group, place),
                        device_id_type=MESH,
                    ).start()

        if first:
            pltpu.make_async_copy(
                source.at[pos, me], target.at[pos, me], own_sems.at[pos]
            ).start()
        for at in range(4):
            send_column(at, first and at == 0)

    def arrived(pos, phase, first, target, sems, own_sems):
        others = target.at[pos, pl.ds(0, devices // PHASES - (1 if first else 0))]
        pltpu.make_async_copy(others, others, sems.at[pos, phase, 1]).wait()
        if first:
            own = target.at[pos, me]
            pltpu.make_async_copy(own, own, own_sems.at[pos]).wait()

    def sent(pos, source, sems):
        def wait(phase, first):
            others = source.at[pos, pl.ds(0, devices // PHASES - (1 if first else 0))]
            pltpu.make_async_copy(others, others, sems.at[pos, phase, 0]).wait()

        in_phases(wait)

    def columns_of(phase):
        return [[near(phase, 2 * two + side) for side in range(2)] for two in twos]

    def pack(phase, first):
        for columns in columns_of(phase):
            sides = [
                features[:, pl.ds(pl.multiple_of(column * 2 * eight, 2 * eight), 2 * eight), :]
                for column in columns
            ]
            left, right = (side.reshape(2 * block, width) for side in sides)
            rows = dot(pack_m[...], halves(left, right)).astype(BF)
            for pos in range(PAIR):
                part = rows[pos * 2 * block : (pos + 1) * 2 * block]
                for side, column in enumerate(columns):
                    send_in[pos, pl.ds(column * eight, eight)] = part[
                        :, side * LANES : (side + 1) * LANES
                    ].reshape(eight, 2 * groups, LANES)
        if first:
            pl.semaphore_wait(barrier, devices - 1)
        exchange(0, phase, first, send_in, recv_in, in_sems, own_in)

    in_phases(pack)
    for pos in range(1, PAIR):
        in_phases(
            lambda phase, first: exchange(pos, phase, first, send_in, recv_in, in_sems, own_in)
        )

    for at in range(len(loads)):
        if at not in first_needed:
            loads[at].wait()

    def select_in(mixture, carry):
        row = lax.broadcasted_iota(jnp.int32, (MAXC, 1), 0)
        pick = jnp.where(row < counts[mixture], row, 0) + offsets[mixture]
        column = lax.broadcasted_iota(jnp.int32, (MAXC, slots), 1)
        gather_m[pl.ds(pl.multiple_of(mixture * MAXC, MAXC), MAXC), :] = jnp.where(column == pick, 1.0, 0.0).astype(BF)
        return carry

    lax.fori_loop(0, MIX, select_in, 0)

    def select_out(step, carry):
        start = pl.multiple_of(step * 2 * block, 2 * block)
        slot = start + lax.broadcasted_iota(jnp.int32, (2 * block, 1), 0)
        pick = jnp.full((2 * block, 1), -1, jnp.int32)
        for mixture in range(MIX):
            place = slot - offsets[mixture]
            inside = (place >= 0) & (place < counts[mixture])
            pick = jnp.where(inside, place + mixture * MAXC, pick)
        column = lax.broadcasted_iota(jnp.int32, (2 * block, MIX * MAXC), 1)
        scatter_m[pl.ds(start, 2 * block), :] = jnp.where(column == pick, 1.0, 0.0).astype(BF)
        return carry

    lax.fori_loop(0, devices // (2 * eight), select_out, 0)
    head = width // HEADS
    scale = math.log2(math.e) / math.sqrt(head)
    wq_t[...] = w_query[...].astype(F32).T.astype(BF)
    wv_t[...] = w_value[...].astype(F32).T.astype(BF)
    column = lax.broadcasted_iota(jnp.int32, (1, MIX * MAXC), 1)
    valid = jnp.zeros((1, MIX * MAXC), F32)
    for mixture in range(MIX):
        inside = (column >= mixture * MAXC) & (column < mixture * MAXC + counts[mixture])
        valid = jnp.where(inside, 1.0, valid)
    is_valid[...] = valid

    def two_blocks(buffer, pos, columns):
        rows = []
        for two in twos:
            sides = [
                buffer[pos, pl.ds(column * eight, eight)].reshape(2 * block, LANES)
                for column in columns[two]
            ]
            rows.append(unhalves(dot(unpack_m[...], jnp.concatenate(sides, axis=1))))
        return rows

    def slots_of(column):
        return pl.ds(pl.multiple_of(column * block, block), block)

    def load(buffer, columns):
        return jnp.concatenate([buffer[slots_of(column), :] for column in columns], axis=0)

    def store(buffer, columns, rows):
        for side, column in enumerate(columns):
            buffer[slots_of(column), :] = rows[side * block : (side + 1) * block]

    def project_keys(mixture, to):
        at = pl.multiple_of(mixture * MAXC, MAXC)
        chosen = normed[pl.ds(at, MAXC), :]
        found = dot(chosen, w_key[...]).astype(BF)
        for half in range(2):
            keys[to][half] = found[:, half * LANES : (half + 1) * LANES]
        query_t[to][...] = (dot_nt(wq_t[...], chosen) * scale).astype(BF)

    def project_values(mixture, to):
        at = pl.multiple_of(mixture * MAXC, MAXC)
        valid = is_valid[:, pl.ds(at, MAXC)]
        value = jnp.where(valid > 0.0, dot_nt(wv_t[...], normed[pl.ds(at, MAXC), :]), 0.0).astype(BF)
        ones = jnp.broadcast_to(valid, (16, MAXC)).astype(BF)
        for h in range(HEADS):
            values_t[to][h, 0:head, :] = value[h * head : (h + 1) * head]
            values_t[to][h, head:, :] = ones

    def scores_of(h, to):
        half, rest = divmod(h * head, LANES)
        lane = lax.broadcasted_iota(jnp.int32, (1, LANES), 1)
        mask = jnp.where((lane >= rest) & (lane < rest + head), 1.0, 0.0).astype(BF)
        queries = query_t[to][half * LANES : (half + 1) * LANES, :]
        logits = dot(keys[to][half] * mask, queries)
        scores[to][h] = logits
        highest[to][h : h + 1, :] = jnp.max(logits, axis=0, keepdims=True)

    def mix_values(mixture, h, to):
        at = pl.multiple_of(mixture * MAXC, MAXC)
        exponent = jnp.exp2(scores[to][h] - highest[to][h : h + 1, :]).astype(BF)
        sums = dot(values_t[to][h], exponent)
        context_t[h * head : (h + 1) * head, pl.ds(at, MAXC)] = (
            sums[:head] / sums[head : head + 1]
        ).astype(BF)

    for pos in range(PAIR):
        def unpack(phase, first):
            arrived(pos, phase, first, recv_in, in_sems, own_in)
            columns = columns_of(phase)
            for two, rows in enumerate(two_blocks(recv_in, pos, columns)):
                store(slots_x, columns[two], rows.astype(BF))
                store(slots_n, columns[two], layer_norm(rows, gain_attn[...]))

        in_phases(unpack)

        def gather(pair, carry):
            places = [
                pl.multiple_of((2 * pair + two) * MAXC, MAXC) for two in range(2)
            ]
            chosen = [dot(gather_m[pl.ds(at, MAXC), :], slots_n[...]) for at in places]
            for at, rows in zip(places, chosen):
                normed[pl.ds(at, MAXC), :] = rows.astype(BF)
            return carry

        lax.fori_loop(0, MIX // 2, gather, 0)
        project_keys(0, 0)
        project_keys(1, 1)
        project_values(0, 0)
        for h in range(HEADS):
            scores_of(h, 0)

        def attend(pair, carry):
            for to in range(2):
                mixture = 2 * pair + to
                for h in range(HEADS):
                    scores_of(h, 1 - to)
                    mix_values(mixture, h, to)
                    if h == 1:
                        project_values(mixture + 1, 1 - to)
                    if h == 4:
                        project_keys(mixture + 2, to)
            return carry

        lax.fori_loop(0, MIX // 2 - 1, attend, 0)
        project_values(MIX - 1, 1)
        for h in range(HEADS):
            scores_of(h, 1)
            mix_values(MIX - 2, h, 0)
        for h in range(HEADS):
            mix_values(MIX - 1, h, 1)

        def combine(phase, first):
            columns = columns_of(phase)
            rows = [dot_nt(load(scatter_m, columns[two]), context_t[...]) for two in twos]
            rows = [dot(row.astype(BF), w_out[...]) for row in rows]
            rows = [
                (row + load(slots_x, columns[two]).astype(F32)).astype(BF)
                for two, row in zip(twos, rows)
            ]
            rows = [dot(repack_m[...], halves(row[:block], row[block:])).astype(BF) for row in rows]
            for two in twos:
                for side in range(2):
                    send_out[pos, pl.ds(columns[two][side] * eight, eight)] = rows[two][
                        :, side * LANES : (side + 1) * LANES
                    ].reshape(eight, 2 * groups, LANES)
            exchange(pos, phase, first, send_out, recv_out, out_sems, own_out)

        in_phases(combine)

    for pos in range(PAIR):

        def finish(phase, first):
            arrived(pos, phase, first, recv_out, out_sems, own_out)
            columns = columns_of(phase)
            rows = two_blocks(recv_out, pos, columns)
            second = [layer_norm(row, gain_ffn[...]) for row in rows]
            for cut in range(0, w_up.shape[1], width):
                for two in twos:
                    hidden[two][:, cut : cut + width] = jnp.maximum(
                        dot(second[two], w_up[:, cut : cut + width]), 0.0
                    ).astype(BF)
            rows = [(rows[two] + dot(hidden[two][...], w_down[...])).astype(BF) for two in twos]
            for two in twos:
                if pos == 0:
                    store(early, columns[two], rows[two])
                    continue
                before = load(early, columns[two])
                for side, column in enumerate(columns[two]):
                    cut = slice(side * block, (side + 1) * block)
                    both = jnp.concatenate([before[cut], rows[two][cut]], axis=0)
                    both = dot(final_m[...], both).astype(BF)
                    place = pl.multiple_of(column * 2 * eight, 2 * eight)
                    here = pl.ds(place, 2 * eight)
                    finished[:, here, :] = both.reshape(groups, 2 * eight, width)
                    pltpu.make_async_copy(
                        finished.at[:, here, :], result.at[:, here, :], done
                    ).start()

        in_phases(finish)

    pltpu.make_async_copy(finished, result, done).wait()
    for pos in range(PAIR):
        sent(pos, send_in, in_sems)
        sent(pos, send_out, out_sems)


def local(
    axis_sizes,
    features,
    gain_attn,
    w_query,
    w_key,
    w_value,
    w_out,
    gain_ffn,
    w_up,
    w_down,
    counts,
    offsets,
):
    groups, positions, width = features.shape
    devices = axis_sizes[0] * axis_sizes[1]
    slots = groups * devices
    matrices = [jnp.asarray(m, BF) for m in permutations(groups, 8)]
    smem = pl.BlockSpec(memory_space=pltpu.SMEM)
    link = pltpu.VMEM((PAIR, devices, 2 * groups, LANES), BF)

    def both(shape):
        return (shape, shape)

    operands = [
        features,
        gain_attn.reshape(1, width),
        w_query,
        w_key,
        w_value,
        w_out,
        gain_ffn.reshape(1, width),
        w_up,
        w_down,
        *matrices,
    ]

    return pl.pallas_call(
        functools.partial(kernel, (devices, axis_sizes)),
        out_shape=jax.ShapeDtypeStruct(features.shape, BF),
        in_specs=[smem, smem] + [pl.BlockSpec(memory_space=pl.ANY)] * 13,
        out_specs=pl.BlockSpec(memory_space=pl.ANY),
        scratch_shapes=[
            pltpu.VMEM(features.shape, BF),
            tuple(pltpu.VMEM(operand.shape, operand.dtype) for operand in operands),
            pltpu.SemaphoreType.DMA((len(operands),)),
            pltpu.SemaphoreType.DMA,
            link,
            link,
            link,
            link,
            pltpu.VMEM((slots, width), BF),
            pltpu.VMEM((slots, width), BF),
            pltpu.VMEM((MIX * MAXC, slots), BF),
            pltpu.VMEM((slots, MIX * MAXC), BF),
            pltpu.VMEM((width, MIX * MAXC), BF),
            pltpu.VMEM((width, width), BF),
            pltpu.VMEM((width, width), BF),
            pltpu.VMEM((1, MIX * MAXC), F32),
            pltpu.VMEM((MIX * MAXC, width), BF),
            both(pltpu.VMEM((width, MAXC), BF)),
            both(pltpu.VMEM((2, MAXC, LANES), BF)),
            both(pltpu.VMEM((HEADS, width // HEADS + 16, MAXC), BF)),
            both(pltpu.VMEM((HEADS, MAXC, MAXC), F32)),
            both(pltpu.VMEM((HEADS, MAXC), F32)),
            both(pltpu.VMEM((16 * groups, w_up.shape[1]), BF)),
            pltpu.VMEM((slots, width), BF),
            pltpu.SemaphoreType.DMA((PAIR, PHASES, 2)),
            pltpu.SemaphoreType.DMA((PAIR, PHASES, 2)),
            pltpu.SemaphoreType.DMA((PAIR,)),
            pltpu.SemaphoreType.DMA((PAIR,)),
        ],
        compiler_params=pltpu.CompilerParams(
            collective_id=0, has_side_effects=True, vmem_limit_bytes=56 << 20
        ),
    )(counts, offsets, *operands)


def solution(mesh):
    axis_sizes = (mesh.shape["group"], mesh.shape["pos"])
    return jax.shard_map(
        functools.partial(local, axis_sizes),
        mesh=mesh,
        in_specs=(P(("group", "pos"), None, None),) + (P(),) * 10,
        out_specs=P(("group", "pos"), None, None),
        check_vma=False,
    )
```

```python
import functools
import math

import jax
import jax.numpy as jnp
import numpy as np
from jax import lax
from jax.experimental import pallas as pl
from jax.experimental.pallas import tpu as pltpu
from jax.sharding import PartitionSpec as P

HEADS = 8
MIX = 6
MAXC = 256
LANES = 128
PAIR = 2
SIDE = 4
PHASES = 4

epsilon = 1e-05
BF = jnp.bfloat16
F32 = jnp.float32
MESH = pl.DeviceIdType.MESH


def one_hot_rows(picks, width):
    matrix = np.zeros((len(picks), width), np.float32)
    matrix[np.arange(len(picks)), picks] = 1.0
    return matrix


def permutations(groups, eight):
    pack = [
        half * groups * 2 * eight + slot * 2 * eight + PAIR * device + pos
        for pos in range(PAIR)
        for device in range(eight)
        for half in range(2)
        for slot in range(groups)
    ]
    unpack = [
        device * 2 * groups + half * groups + slot
        for half in range(2)
        for device in range(eight)
        for slot in range(groups)
    ]
    final = [
        pos * eight * groups + device * groups + slot
        for slot in range(groups)
        for device in range(eight)
        for pos in range(PAIR)
    ]
    unpack_matrix = one_hot_rows(unpack, 2 * eight * groups)
    return (
        one_hot_rows(pack, 2 * 2 * eight * groups),
        unpack_matrix,
        unpack_matrix.T.copy(),
        one_hot_rows(final, PAIR * eight * groups),
    )


def dot(left, right):
    return jnp.dot(left, right, preferred_element_type=F32)


def dot_nt(left, right):
    return lax.dot_general(
        left, right, (((1,), (1,)), ((), ())), preferred_element_type=F32
    )


def layer_norm(floats, gain):
    average = jnp.mean(floats, axis=-1, keepdims=True)
    centred = floats - average
    spread = jnp.mean(centred * centred, axis=-1, keepdims=True)
    return (centred * lax.rsqrt(spread + epsilon) * gain).astype(BF)


def halves(left, right):
    low = jnp.concatenate([left[:, :LANES], right[:, :LANES]], axis=1)
    high = jnp.concatenate([left[:, LANES:], right[:, LANES:]], axis=1)
    return jnp.concatenate([low, high], axis=0)


def unhalves(rows):
    count = rows.shape[0] // 2
    left = jnp.concatenate([rows[:count, :LANES], rows[count:, :LANES]], axis=1)
    right = jnp.concatenate([rows[:count, LANES:], rows[count:, LANES:]], axis=1)
    return jnp.concatenate([left, right], axis=0)


def kernel(
    sizes,
    counts,
    offsets,
    *refs,
):
    operands, (result, staged, load_sems), rest = refs[:13], refs[13:16], refs[16:]
    (
        features,
        gain_attn,
        w_query,
        w_key,
        w_value,
        w_out,
        gain_ffn,
        w_up,
        w_down,
        pack_m,
        unpack_m,
        repack_m,
        final_m,
    ) = staged
    (
        send_in,
        recv_in,
        send_out,
        recv_out,
        slots_x,
        slots_n,
        gather_m,
        scatter_m,
        context_t,
        wq_t,
        wv_t,
        is_valid,
        normed,
        query_t,
        keys,
        values_t,
        scores,
        highest,
        hidden,
        early,
        in_sems,
        out_sems,
        own_in,
        own_out,
    ) = rest
    devices, axis_sizes = sizes
    groups = features.shape[0]
    width = features.shape[2]
    slots = devices * groups
    eight = 8
    block = eight * groups
    wide = 4
    twos = range(wide // 2)
    assert devices == PHASES * wide * eight
    group_at = lax.axis_index("group")
    pos_at = lax.axis_index("pos")
    me = group_at * axis_sizes[1] + pos_at
    cores = axis_sizes[0] // (SIDE * SIDE)
    y_at = group_at // (SIDE * cores)
    x_at = lax.rem(group_at // cores, SIDE)
    core_at = lax.rem(group_at, cores)

    loads = [
        pltpu.make_async_copy(operand, place, load_sems.at[at])
        for at, (operand, place) in enumerate(zip(operands, staged))
    ]
    first_needed = (0, 9)
    for at in first_needed:
        loads[at].start()
    barrier = pltpu.get_barrier_semaphore()

    along = [lax.rem(pos_at + hop, axis_sizes[1]) for hop in range(axis_sizes[1])]

    def greet(group, place):
        pl.semaphore_signal(barrier, inc=1, device_id=(group, place), device_id_type=MESH)

    def greet_group(step, carry):
        for place in along:
            greet(lax.rem(group_at + step, axis_sizes[0]), place)
        return carry

    for place in along[1:]:
        greet(group_at, place)
    lax.fori_loop(1, axis_sizes[0], greet_group, 0)

    for at in range(len(loads)):
        if at not in first_needed:
            loads[at].start()
    for at in first_needed:
        loads[at].wait()

    def near(phase, at):
        y = lax.rem(y_at + phase // 2 + 2 * (at // 2), SIDE)
        x = lax.rem(x_at + phase % 2 + 2 * (at % 2), SIDE)
        return y * SIDE + x

    def in_phases(body):
        body(0, True)

        def later(phase, carry):
            body(phase, False)
            return carry

        lax.fori_loop(1, PHASES, later, 0)

    def exchange(pos, phase, first, source, target, sems, own_sems):
        def send_column(at, skip):
            column = near(phase, at)
            for core in range(cores):
                for hop in range(axis_sizes[1]):
                    if skip and core == 0 and hop == 0:
                        continue
                    group = column * cores + lax.rem(core_at + core, cores)
                    place = along[hop]
                    pltpu.make_async_remote_copy(
                        src_ref=source.at[pos, group * axis_sizes[1] + place],
                        dst_ref=target.at[pos, me],
                        send_sem=sems.at[pos, phase, 0],
                        recv_sem=sems.at[pos, phase, 1],
                        device_id=(group, place),
                        device_id_type=MESH,
                    ).start()

        if first:
            pltpu.make_async_copy(
                source.at[pos, me], target.at[pos, me], own_sems.at[pos]
            ).start()
        for at in range(4):
            send_column(at, first and at == 0)

    def arrived(pos, phase, first, target, sems, own_sems):
        others = target.at[pos, pl.ds(0, devices // PHASES - (1 if first else 0))]
        pltpu.make_async_copy(others, others, sems.at[pos, phase, 1]).wait()
        if first:
            own = target.at[pos, me]
            pltpu.make_async_copy(own, own, own_sems.at[pos]).wait()

    def sent(pos, source, sems):
        def wait(phase, first):
            others = source.at[pos, pl.ds(0, devices // PHASES - (1 if first else 0))]
            pltpu.make_async_copy(others, others, sems.at[pos, phase, 0]).wait()

        in_phases(wait)

    def columns_of(phase):
        return [[near(phase, 2 * two + side) for side in range(2)] for two in twos]

    def pack(phase, first):
        for columns in columns_of(phase):
            sides = [
                features[:, pl.ds(pl.multiple_of(column * 2 * eight, 2 * eight), 2 * eight), :]
                for column in columns
            ]
            left, right = (side.reshape(2 * block, width) for side in sides)
            rows = dot(pack_m[...], halves(left, right)).astype(BF)
            for pos in range(PAIR):
                part = rows[pos * 2 * block : (pos + 1) * 2 * block]
                for side, column in enumerate(columns):
                    send_in[pos, pl.ds(column * eight, eight)] = part[
                        :, side * LANES : (side + 1) * LANES
                    ].reshape(eight, 2 * groups, LANES)
        if first:
            pl.semaphore_wait(barrier, devices - 1)
        exchange(0, phase, first, send_in, recv_in, in_sems, own_in)

    in_phases(pack)
    for pos in range(1, PAIR):
        in_phases(
            lambda phase, first: exchange(pos, phase, first, send_in, recv_in, in_sems, own_in)
        )

    for at in range(len(loads)):
        if at not in first_needed:
            loads[at].wait()

    def select_in(mixture, carry):
        row = lax.broadcasted_iota(jnp.int32, (MAXC, 1), 0)
        pick = jnp.where(row < counts[mixture], row, 0) + offsets[mixture]
        column = lax.broadcasted_iota(jnp.int32, (MAXC, slots), 1)
        gather_m[pl.ds(pl.multiple_of(mixture * MAXC, MAXC), MAXC), :] = jnp.where(column == pick, 1.0, 0.0).astype(BF)
        return carry

    lax.fori_loop(0, MIX, select_in, 0)

    def select_out(step, carry):
        start = pl.multiple_of(step * 2 * block, 2 * block)
        slot = start + lax.broadcasted_iota(jnp.int32, (2 * block, 1), 0)
        pick = jnp.full((2 * block, 1), -1, jnp.int32)
        for mixture in range(MIX):
            place = slot - offsets[mixture]
            inside = (place >= 0) & (place < counts[mixture])
            pick = jnp.where(inside, place + mixture * MAXC, pick)
        column = lax.broadcasted_iota(jnp.int32, (2 * block, MIX * MAXC), 1)
        scatter_m[pl.ds(start, 2 * block), :] = jnp.where(column == pick, 1.0, 0.0).astype(BF)
        return carry

    lax.fori_loop(0, devices // (2 * eight), select_out, 0)
    head = width // HEADS
    scale = math.log2(math.e) / math.sqrt(head)
    wq_t[...] = w_query[...].astype(F32).T.astype(BF)
    wv_t[...] = w_value[...].astype(F32).T.astype(BF)
    column = lax.broadcasted_iota(jnp.int32, (1, MIX * MAXC), 1)
    valid = jnp.zeros((1, MIX * MAXC), F32)
    for mixture in range(MIX):
        inside = (column >= mixture * MAXC) & (column < mixture * MAXC + counts[mixture])
        valid = jnp.where(inside, 1.0, valid)
    is_valid[...] = valid

    def two_blocks(buffer, pos, columns):
        rows = []
        for two in twos:
            sides = [
                buffer[pos, pl.ds(column * eight, eight)].reshape(2 * block, LANES)
                for column in columns[two]
            ]
            rows.append(unhalves(dot(unpack_m[...], jnp.concatenate(sides, axis=1))))
        return rows

    def slots_of(column):
        return pl.ds(pl.multiple_of(column * block, block), block)

    def load(buffer, columns):
        return jnp.concatenate([buffer[slots_of(column), :] for column in columns], axis=0)

    def store(buffer, columns, rows):
        for side, column in enumerate(columns):
            buffer[slots_of(column), :] = rows[side * block : (side + 1) * block]

    def project_keys(mixture, to):
        at = pl.multiple_of(mixture * MAXC, MAXC)
        chosen = normed[pl.ds(at, MAXC), :]
        found = dot(chosen, w_key[...]).astype(BF)
        for half in range(2):
            keys[to][half] = found[:, half * LANES : (half + 1) * LANES]
        query_t[to][...] = (dot_nt(wq_t[...], chosen) * scale).astype(BF)

    def project_values(mixture, to):
        at = pl.multiple_of(mixture * MAXC, MAXC)
        valid = is_valid[:, pl.ds(at, MAXC)]
        value = jnp.where(valid > 0.0, dot_nt(wv_t[...], normed[pl.ds(at, MAXC), :]), 0.0).astype(BF)
        ones = jnp.broadcast_to(valid, (16, MAXC)).astype(BF)
        for h in range(HEADS):
            values_t[to][h, 0:head, :] = value[h * head : (h + 1) * head]
            values_t[to][h, head:, :] = ones

    def scores_of(h, to):
        half, rest = divmod(h * head, LANES)
        lane = lax.broadcasted_iota(jnp.int32, (1, LANES), 1)
        mask = jnp.where((lane >= rest) & (lane < rest + head), 1.0, 0.0).astype(BF)
        queries = query_t[to][half * LANES : (half + 1) * LANES, :]
        logits = dot(keys[to][half] * mask, queries)
        scores[to][h] = logits
        highest[to][h : h + 1, :] = jnp.max(logits, axis=0, keepdims=True)

    def mix_values(mixture, h, to):
        at = pl.multiple_of(mixture * MAXC, MAXC)
        exponent = jnp.exp2(scores[to][h] - highest[to][h : h + 1, :]).astype(BF)
        sums = dot(values_t[to][h], exponent)
        context_t[h * head : (h + 1) * head, pl.ds(at, MAXC)] = (
            sums[:head] / sums[head : head + 1]
        ).astype(BF)

    for pos in range(PAIR):
        def unpack(phase, first):
            arrived(pos, phase, first, recv_in, in_sems, own_in)
            columns = columns_of(phase)
            for two, rows in enumerate(two_blocks(recv_in, pos, columns)):
                store(slots_x, columns[two], rows.astype(BF))
                store(slots_n, columns[two], layer_norm(rows, gain_attn[...]))

        in_phases(unpack)

        def gather(mixture):
            at = mixture * MAXC
            chosen = dot(gather_m[at : at + MAXC, :], slots_n[...])
            normed[at : at + MAXC, :] = chosen.astype(BF)

        for mixture in range(2):
            gather(mixture)
        project_keys(0, 0)
        for mixture in range(2, 4):
            gather(mixture)
        project_values(0, 0)
        project_keys(1, 1)
        for h in range(HEADS):
            scores_of(h, 0)
            if h in (1, 4):
                gather(4 + h // 4)

        def attend(pair, carry):
            for to in range(2):
                mixture = 2 * pair + to
                for h in range(HEADS):
                    scores_of(h, 1 - to)
                    mix_values(mixture, h, to)
                    if h == 1:
                        project_values(mixture + 1, 1 - to)
                    if h == 4:
                        project_keys(mixture + 2, to)
            return carry

        lax.fori_loop(0, MIX // 2 - 1, attend, 0)
        project_values(MIX - 1, 1)
        for h in range(HEADS):
            scores_of(h, 1)
            mix_values(MIX - 2, h, 0)
        for h in range(HEADS):
            mix_values(MIX - 1, h, 1)

        def combine(phase, first):
            columns = columns_of(phase)
            rows = [dot_nt(load(scatter_m, columns[two]), context_t[...]) for two in twos]
            rows = [dot(row.astype(BF), w_out[...]) for row in rows]
            rows = [
                (row + load(slots_x, columns[two]).astype(F32)).astype(BF)
                for two, row in zip(twos, rows)
            ]
            rows = [dot(repack_m[...], halves(row[:block], row[block:])).astype(BF) for row in rows]
            for two in twos:
                for side in range(2):
                    send_out[pos, pl.ds(columns[two][side] * eight, eight)] = rows[two][
                        :, side * LANES : (side + 1) * LANES
                    ].reshape(eight, 2 * groups, LANES)
            exchange(pos, phase, first, send_out, recv_out, out_sems, own_out)

        in_phases(combine)

    for pos in range(PAIR):

        def finish(phase, first):
            arrived(pos, phase, first, recv_out, out_sems, own_out)
            columns = columns_of(phase)
            rows = two_blocks(recv_out, pos, columns)
            second = [layer_norm(row, gain_ffn[...]) for row in rows]
            for cut in range(0, w_up.shape[1], width):
                for two in twos:
                    hidden[two][:, cut : cut + width] = jnp.maximum(
                        dot(second[two], w_up[:, cut : cut + width]), 0.0
                    ).astype(BF)
            rows = [(rows[two] + dot(hidden[two][...], w_down[...])).astype(BF) for two in twos]
            for two in twos:
                if pos == 0:
                    store(early, columns[two], rows[two])
                    continue
                before = load(early, columns[two])
                for side, column in enumerate(columns[two]):
                    cut = slice(side * block, (side + 1) * block)
                    both = jnp.concatenate([before[cut], rows[two][cut]], axis=0)
                    both = dot(final_m[...], both).astype(BF)
                    place = pl.multiple_of(column * 2 * eight, 2 * eight)
                    here = pl.ds(place, 2 * eight)
                    result[:, here, :] = both.reshape(groups, 2 * eight, width)

        in_phases(finish)

    for pos in range(PAIR):
        sent(pos, send_in, in_sems)
        sent(pos, send_out, out_sems)


def local(
    axis_sizes,
    features,
    gain_attn,
    w_query,
    w_key,
    w_value,
    w_out,
    gain_ffn,
    w_up,
    w_down,
    counts,
    offsets,
):
    groups, positions, width = features.shape
    devices = axis_sizes[0] * axis_sizes[1]
    slots = groups * devices
    matrices = [jnp.asarray(m, BF) for m in permutations(groups, 8)]
    smem = pl.BlockSpec(memory_space=pltpu.SMEM)
    link = pltpu.VMEM((PAIR, devices, 2 * groups, LANES), BF)

    def both(shape):
        return (shape, shape)

    operands = [
        features,
        gain_attn.reshape(1, width),
        w_query,
        w_key,
        w_value,
        w_out,
        gain_ffn.reshape(1, width),
        w_up,
        w_down,
        *matrices,
    ]

    return pl.pallas_call(
        functools.partial(kernel, (devices, axis_sizes)),
        out_shape=pltpu.VMEM(features.shape, BF),
        in_specs=[smem, smem] + [pl.BlockSpec(memory_space=pl.ANY)] * 13,
        out_specs=pl.BlockSpec(memory_space=pltpu.VMEM),
        scratch_shapes=[
            tuple(pltpu.VMEM(operand.shape, operand.dtype) for operand in operands),
            pltpu.SemaphoreType.DMA((len(operands),)),
            link,
            link,
            link,
            link,
            pltpu.VMEM((slots, width), BF),
            pltpu.VMEM((slots, width), BF),
            pltpu.VMEM((MIX * MAXC, slots), BF),
            pltpu.VMEM((slots, MIX * MAXC), BF),
            pltpu.VMEM((width, MIX * MAXC), BF),
            pltpu.VMEM((width, width), BF),
            pltpu.VMEM((width, width), BF),
            pltpu.VMEM((1, MIX * MAXC), F32),
            pltpu.VMEM((MIX * MAXC, width), BF),
            both(pltpu.VMEM((width, MAXC), BF)),
            both(pltpu.VMEM((2, MAXC, LANES), BF)),
            both(pltpu.VMEM((HEADS, width // HEADS + 16, MAXC), BF)),
            both(pltpu.VMEM((HEADS, MAXC, MAXC), F32)),
            both(pltpu.VMEM((HEADS, MAXC), F32)),
            both(pltpu.VMEM((16 * groups, w_up.shape[1]), BF)),
            pltpu.VMEM((slots, width), BF),
            pltpu.SemaphoreType.DMA((PAIR, PHASES, 2)),
            pltpu.SemaphoreType.DMA((PAIR, PHASES, 2)),
            pltpu.SemaphoreType.DMA((PAIR,)),
            pltpu.SemaphoreType.DMA((PAIR,)),
        ],
        compiler_params=pltpu.CompilerParams(
            collective_id=0, has_side_effects=True, vmem_limit_bytes=56 << 20
        ),
    )(counts, offsets, *operands)


def solution(mesh):
    axis_sizes = (mesh.shape["group"], mesh.shape["pos"])
    return jax.shard_map(
        functools.partial(local, axis_sizes),
        mesh=mesh,
        in_specs=(P(("group", "pos"), None, None),) + (P(),) * 10,
        out_specs=P(("group", "pos"), None, None),
        check_vma=False,
    )
```

```python
import functools
import math

import jax
import jax.numpy as jnp
import numpy as np
from jax import lax
from jax.experimental import pallas as pl
from jax.experimental.pallas import tpu as pltpu
from jax.sharding import PartitionSpec as P

HEADS = 8
MIX = 6
MAXC = 256
LANES = 128
PAIR = 2
SIDE = 4
PHASES = 4

epsilon = 1e-05
BF = jnp.bfloat16
F32 = jnp.float32
MESH = pl.DeviceIdType.MESH


def one_hot_rows(picks, width):
    matrix = np.zeros((len(picks), width), np.float32)
    matrix[np.arange(len(picks)), picks] = 1.0
    return matrix


def permutations(groups, eight):
    pack = [
        half * groups * 2 * eight + slot * 2 * eight + PAIR * device + pos
        for pos in range(PAIR)
        for device in range(eight)
        for half in range(2)
        for slot in range(groups)
    ]
    unpack = [
        device * 2 * groups + half * groups + slot
        for half in range(2)
        for device in range(eight)
        for slot in range(groups)
    ]
    final = [
        pos * eight * groups + device * groups + slot
        for slot in range(groups)
        for device in range(eight)
        for pos in range(PAIR)
    ]
    unpack_matrix = one_hot_rows(unpack, 2 * eight * groups)
    return (
        one_hot_rows(pack, 2 * 2 * eight * groups),
        unpack_matrix,
        unpack_matrix.T.copy(),
        one_hot_rows(final, PAIR * eight * groups),
    )


def dot(left, right):
    return jnp.dot(left, right, preferred_element_type=F32)


def dot_nt(left, right):
    return lax.dot_general(
        left, right, (((1,), (1,)), ((), ())), preferred_element_type=F32
    )


def layer_norm(floats, gain):
    average = jnp.mean(floats, axis=-1, keepdims=True)
    centred = floats - average
    spread = jnp.mean(centred * centred, axis=-1, keepdims=True)
    return (centred * lax.rsqrt(spread + epsilon) * gain).astype(BF)


def halves(left, right):
    low = jnp.concatenate([left[:, :LANES], right[:, :LANES]], axis=1)
    high = jnp.concatenate([left[:, LANES:], right[:, LANES:]], axis=1)
    return jnp.concatenate([low, high], axis=0)


def unhalves(rows):
    count = rows.shape[0] // 2
    left = jnp.concatenate([rows[:count, :LANES], rows[count:, :LANES]], axis=1)
    right = jnp.concatenate([rows[:count, LANES:], rows[count:, LANES:]], axis=1)
    return jnp.concatenate([left, right], axis=0)


def kernel(
    sizes,
    counts,
    offsets,
    *refs,
):
    operands, (result, staged, load_sems), rest = refs[:13], refs[13:16], refs[16:]
    (
        features,
        gain_attn,
        w_query,
        w_key,
        w_value,
        w_out,
        gain_ffn,
        w_up,
        w_down,
        pack_m,
        unpack_m,
        repack_m,
        final_m,
    ) = staged
    (
        send_in,
        recv_in,
        send_out,
        recv_out,
        slots_x,
        slots_n,
        gather_m,
        scatter_m,
        context_t,
        wq_t,
        wv_t,
        is_valid,
        normed,
        query_t,
        keys,
        values_t,
        scores,
        highest,
        hidden,
        early,
        in_sems,
        out_sems,
        own_in,
        own_out,
    ) = rest
    devices, axis_sizes = sizes
    groups = features.shape[0]
    width = features.shape[2]
    slots = devices * groups
    eight = 8
    block = eight * groups
    wide = 4
    twos = range(wide // 2)
    assert devices == PHASES * wide * eight
    group_at = lax.axis_index("group")
    pos_at = lax.axis_index("pos")
    me = group_at * axis_sizes[1] + pos_at
    cores = axis_sizes[0] // (SIDE * SIDE)
    y_at = group_at // (SIDE * cores)
    x_at = lax.rem(group_at // cores, SIDE)
    core_at = lax.rem(group_at, cores)

    loads = [
        pltpu.make_async_copy(operand, place, load_sems.at[at])
        for at, (operand, place) in enumerate(zip(operands, staged))
    ]
    first_needed = (0, 9)
    for at in first_needed:
        loads[at].start()
    barrier = pltpu.get_barrier_semaphore()

    along = [lax.rem(pos_at + hop, axis_sizes[1]) for hop in range(axis_sizes[1])]

    def greet(group, place):
        pl.semaphore_signal(barrier, inc=1, device_id=(group, place), device_id_type=MESH)

    def greet_group(step, carry):
        for place in along:
            greet(lax.rem(group_at + step, axis_sizes[0]), place)
        return carry

    for place in along[1:]:
        greet(group_at, place)
    lax.fori_loop(1, axis_sizes[0], greet_group, 0)

    for at in range(len(loads)):
        if at not in first_needed:
            loads[at].start()
    for at in first_needed:
        loads[at].wait()

    def near(phase, at):
        y = lax.rem(y_at + phase // 2 + 2 * (at // 2), SIDE)
        x = lax.rem(x_at + phase % 2 + 2 * (at % 2), SIDE)
        return y * SIDE + x

    def in_phases(body):
        body(0, True)

        def later(phase, carry):
            body(phase, False)
            return carry

        lax.fori_loop(1, PHASES, later, 0)

    def exchange(pos, phase, first, source, target, sems, own_sems):
        def send_column(at, skip):
            column = near(phase, at)
            for core in range(cores):
                for hop in range(axis_sizes[1]):
                    if skip and core == 0 and hop == 0:
                        continue
                    group = column * cores + lax.rem(core_at + core, cores)
                    place = along[hop]
                    pltpu.make_async_remote_copy(
                        src_ref=source.at[pos, group * axis_sizes[1] + place],
                        dst_ref=target.at[pos, me],
                        send_sem=sems.at[pos, phase, 0],
                        recv_sem=sems.at[pos, phase, 1],
                        device_id=(group, place),
                        device_id_type=MESH,
                    ).start()

        if first:
            pltpu.make_async_copy(
                source.at[pos, me], target.at[pos, me], own_sems.at[pos]
            ).start()
        for at in range(4):
            send_column(at, first and at == 0)

    def arrived(pos, phase, first, target, sems, own_sems):
        others = target.at[pos, pl.ds(0, devices // PHASES - (1 if first else 0))]
        pltpu.make_async_copy(others, others, sems.at[pos, phase, 1]).wait()
        if first:
            own = target.at[pos, me]
            pltpu.make_async_copy(own, own, own_sems.at[pos]).wait()

    def sent(pos, source, sems):
        def wait(phase, first):
            others = source.at[pos, pl.ds(0, devices // PHASES - (1 if first else 0))]
            pltpu.make_async_copy(others, others, sems.at[pos, phase, 0]).wait()

        in_phases(wait)

    def columns_of(phase):
        return [[near(phase, 2 * two + side) for side in range(2)] for two in twos]

    def pack(phase, first):
        for columns in columns_of(phase):
            sides = [
                features[:, pl.ds(pl.multiple_of(column * 2 * eight, 2 * eight), 2 * eight), :]
                for column in columns
            ]
            left, right = (side.reshape(2 * block, width) for side in sides)
            rows = dot(pack_m[...], halves(left, right)).astype(BF)
            for pos in range(PAIR):
                part = rows[pos * 2 * block : (pos + 1) * 2 * block]
                for side, column in enumerate(columns):
                    send_in[pos, pl.ds(column * eight, eight)] = part[
                        :, side * LANES : (side + 1) * LANES
                    ].reshape(eight, 2 * groups, LANES)
        if first:
            pl.semaphore_wait(barrier, devices - 1)
        exchange(0, phase, first, send_in, recv_in, in_sems, own_in)

    in_phases(pack)
    for pos in range(1, PAIR):
        in_phases(
            lambda phase, first: exchange(pos, phase, first, send_in, recv_in, in_sems, own_in)
        )

    for at in range(len(loads)):
        if at not in first_needed:
            loads[at].wait()

    def select_in(mixture, carry):
        row = lax.broadcasted_iota(jnp.int32, (MAXC, 1), 0)
        pick = jnp.where(row < counts[mixture], row, 0) + offsets[mixture]
        column = lax.broadcasted_iota(jnp.int32, (MAXC, slots), 1)
        gather_m[pl.ds(pl.multiple_of(mixture * MAXC, MAXC), MAXC), :] = jnp.where(column == pick, 1.0, 0.0).astype(BF)
        return carry

    lax.fori_loop(0, MIX, select_in, 0)

    def select_out(step, carry):
        start = pl.multiple_of(step * 2 * block, 2 * block)
        slot = start + lax.broadcasted_iota(jnp.int32, (2 * block, 1), 0)
        pick = jnp.full((2 * block, 1), -1, jnp.int32)
        for mixture in range(MIX):
            place = slot - offsets[mixture]
            inside = (place >= 0) & (place < counts[mixture])
            pick = jnp.where(inside, place + mixture * MAXC, pick)
        column = lax.broadcasted_iota(jnp.int32, (2 * block, MIX * MAXC), 1)
        scatter_m[pl.ds(start, 2 * block), :] = jnp.where(column == pick, 1.0, 0.0).astype(BF)
        return carry

    lax.fori_loop(0, devices // (2 * eight), select_out, 0)
    head = width // HEADS
    scale = math.log2(math.e) / math.sqrt(head)
    wq_t[...] = w_query[...].astype(F32).T.astype(BF)
    wv_t[...] = w_value[...].astype(F32).T.astype(BF)
    column = lax.broadcasted_iota(jnp.int32, (1, MIX * MAXC), 1)
    valid = jnp.zeros((1, MIX * MAXC), F32)
    for mixture in range(MIX):
        inside = (column >= mixture * MAXC) & (column < mixture * MAXC + counts[mixture])
        valid = jnp.where(inside, 1.0, valid)
    is_valid[...] = valid

    def two_blocks(buffer, pos, columns):
        rows = []
        for two in twos:
            sides = [
                buffer[pos, pl.ds(column * eight, eight)].reshape(2 * block, LANES)
                for column in columns[two]
            ]
            rows.append(unhalves(dot(unpack_m[...], jnp.concatenate(sides, axis=1))))
        return rows

    def slots_of(column):
        return pl.ds(pl.multiple_of(column * block, block), block)

    def load(buffer, columns):
        return jnp.concatenate([buffer[slots_of(column), :] for column in columns], axis=0)

    def store(buffer, columns, rows):
        for side, column in enumerate(columns):
            buffer[slots_of(column), :] = rows[side * block : (side + 1) * block]

    def project_keys(mixture, to):
        at = mixture * MAXC
        chosen = normed[pl.ds(at, MAXC), :]
        found = dot(chosen, w_key[...]).astype(BF)
        for half in range(2):
            keys[to][half] = found[:, half * LANES : (half + 1) * LANES]
        query_t[to][...] = (dot_nt(wq_t[...], chosen) * scale).astype(BF)

    def project_values(mixture, to):
        at = mixture * MAXC
        valid = is_valid[:, pl.ds(at, MAXC)]
        value = jnp.where(valid > 0.0, dot_nt(wv_t[...], normed[pl.ds(at, MAXC), :]), 0.0).astype(BF)
        ones = jnp.broadcast_to(valid, (16, MAXC)).astype(BF)
        for h in range(HEADS):
            values_t[to][h, 0:head, :] = value[h * head : (h + 1) * head]
            values_t[to][h, head:, :] = ones

    def scores_of(h, to):
        half, rest = divmod(h * head, LANES)
        lane = lax.broadcasted_iota(jnp.int32, (1, LANES), 1)
        mask = jnp.where((lane >= rest) & (lane < rest + head), 1.0, 0.0).astype(BF)
        queries = query_t[to][half * LANES : (half + 1) * LANES, :]
        logits = dot(keys[to][half] * mask, queries)
        scores[to][h] = logits
        highest[to][h : h + 1, :] = jnp.max(logits, axis=0, keepdims=True)

    def mix_values(mixture, h, to):
        at = mixture * MAXC
        exponent = jnp.exp2(scores[to][h] - highest[to][h : h + 1, :]).astype(BF)
        sums = dot(values_t[to][h], exponent)
        context_t[h * head : (h + 1) * head, pl.ds(at, MAXC)] = (
            sums[:head] / sums[head : head + 1]
        ).astype(BF)

    for pos in range(PAIR):
        def unpack(phase, first):
            arrived(pos, phase, first, recv_in, in_sems, own_in)
            columns = columns_of(phase)
            for two, rows in enumerate(two_blocks(recv_in, pos, columns)):
                store(slots_x, columns[two], rows.astype(BF))
                store(slots_n, columns[two], layer_norm(rows, gain_attn[...]))

        in_phases(unpack)

        def gather(mixture):
            at = mixture * MAXC
            chosen = dot(gather_m[at : at + MAXC, :], slots_n[...])
            normed[at : at + MAXC, :] = chosen.astype(BF)

        for mixture in range(2):
            gather(mixture)
        project_keys(0, 0)
        for mixture in range(2, 4):
            gather(mixture)
        project_values(0, 0)
        project_keys(1, 1)
        for h in range(HEADS):
            scores_of(h, 0)
            if h in (1, 4):
                gather(4 + h // 4)

        def attend(pair, carry):
            for to in range(2):
                mixture = 2 * pair + to
                for h in range(HEADS):
                    scores_of(h, 1 - to)
                    mix_values(mixture, h, to)
                    if h == 1:
                        project_values(mixture + 1, 1 - to)
                    if h == 4:
                        project_keys(mixture + 2, to)
            return carry

        for pair in range(MIX // 2 - 1):
            attend(pair, 0)
        project_values(MIX - 1, 1)
        for h in range(HEADS):
            scores_of(h, 1)
            mix_values(MIX - 2, h, 0)
        for h in range(HEADS):
            mix_values(MIX - 1, h, 1)

        def combine(phase, first):
            columns = columns_of(phase)
            rows = [dot_nt(load(scatter_m, columns[two]), context_t[...]) for two in twos]
            rows = [dot(row.astype(BF), w_out[...]) for row in rows]
            rows = [
                (row + load(slots_x, columns[two]).astype(F32)).astype(BF)
                for two, row in zip(twos, rows)
            ]
            rows = [dot(repack_m[...], halves(row[:block], row[block:])).astype(BF) for row in rows]
            for two in twos:
                for side in range(2):
                    send_out[pos, pl.ds(columns[two][side] * eight, eight)] = rows[two][
                        :, side * LANES : (side + 1) * LANES
                    ].reshape(eight, 2 * groups, LANES)
            exchange(pos, phase, first, send_out, recv_out, out_sems, own_out)

        in_phases(combine)

    for pos in range(PAIR):

        def finish(phase, first):
            arrived(pos, phase, first, recv_out, out_sems, own_out)
            columns = columns_of(phase)
            rows = two_blocks(recv_out, pos, columns)
            second = [layer_norm(row, gain_ffn[...]) for row in rows]
            for cut in range(0, w_up.shape[1], width):
                for two in twos:
                    hidden[two][:, cut : cut + width] = jnp.maximum(
                        dot(second[two], w_up[:, cut : cut + width]), 0.0
                    ).astype(BF)
            rows = [(rows[two] + dot(hidden[two][...], w_down[...])).astype(BF) for two in twos]
            for two in twos:
                if pos == 0:
                    store(early, columns[two], rows[two])
                    continue
                before = load(early, columns[two])
                for side, column in enumerate(columns[two]):
                    cut = slice(side * block, (side + 1) * block)
                    both = jnp.concatenate([before[cut], rows[two][cut]], axis=0)
                    both = dot(final_m[...], both).astype(BF)
                    place = pl.multiple_of(column * 2 * eight, 2 * eight)
                    here = pl.ds(place, 2 * eight)
                    result[:, here, :] = both.reshape(groups, 2 * eight, width)

        in_phases(finish)

    for pos in range(PAIR):
        sent(pos, send_in, in_sems)
        sent(pos, send_out, out_sems)


def local(
    axis_sizes,
    features,
    gain_attn,
    w_query,
    w_key,
    w_value,
    w_out,
    gain_ffn,
    w_up,
    w_down,
    counts,
    offsets,
):
    groups, positions, width = features.shape
    devices = axis_sizes[0] * axis_sizes[1]
    slots = groups * devices
    matrices = [jnp.asarray(m, BF) for m in permutations(groups, 8)]
    smem = pl.BlockSpec(memory_space=pltpu.SMEM)
    link = pltpu.VMEM((PAIR, devices, 2 * groups, LANES), BF)

    def both(shape):
        return (shape, shape)

    operands = [
        features,
        gain_attn.reshape(1, width),
        w_query,
        w_key,
        w_value,
        w_out,
        gain_ffn.reshape(1, width),
        w_up,
        w_down,
        *matrices,
    ]

    return pl.pallas_call(
        functools.partial(kernel, (devices, axis_sizes)),
        out_shape=pltpu.VMEM(features.shape, BF),
        in_specs=[smem, smem] + [pl.BlockSpec(memory_space=pl.ANY)] * 13,
        out_specs=pl.BlockSpec(memory_space=pltpu.VMEM),
        scratch_shapes=[
            tuple(pltpu.VMEM(operand.shape, operand.dtype) for operand in operands),
            pltpu.SemaphoreType.DMA((len(operands),)),
            link,
            link,
            link,
            link,
            pltpu.VMEM((slots, width), BF),
            pltpu.VMEM((slots, width), BF),
            pltpu.VMEM((MIX * MAXC, slots), BF),
            pltpu.VMEM((slots, MIX * MAXC), BF),
            pltpu.VMEM((width, MIX * MAXC), BF),
            pltpu.VMEM((width, width), BF),
            pltpu.VMEM((width, width), BF),
            pltpu.VMEM((1, MIX * MAXC), F32),
            pltpu.VMEM((MIX * MAXC, width), BF),
            both(pltpu.VMEM((width, MAXC), BF)),
            both(pltpu.VMEM((2, MAXC, LANES), BF)),
            both(pltpu.VMEM((HEADS, width // HEADS + 16, MAXC), BF)),
            both(pltpu.VMEM((HEADS, MAXC, MAXC), F32)),
            both(pltpu.VMEM((HEADS, MAXC), F32)),
            both(pltpu.VMEM((16 * groups, w_up.shape[1]), BF)),
            pltpu.VMEM((slots, width), BF),
            pltpu.SemaphoreType.DMA((PAIR, PHASES, 2)),
            pltpu.SemaphoreType.DMA((PAIR, PHASES, 2)),
            pltpu.SemaphoreType.DMA((PAIR,)),
            pltpu.SemaphoreType.DMA((PAIR,)),
        ],
        compiler_params=pltpu.CompilerParams(
            collective_id=0, has_side_effects=True, vmem_limit_bytes=56 << 20
        ),
    )(counts, offsets, *operands)


def solution(mesh):
    axis_sizes = (mesh.shape["group"], mesh.shape["pos"])
    return jax.shard_map(
        functools.partial(local, axis_sizes),
        mesh=mesh,
        in_specs=(P(("group", "pos"), None, None),) + (P(),) * 10,
        out_specs=P(("group", "pos"), None, None),
        check_vma=False,
    )
```
